32 devices in a mesh: section: 2 (over core), dp: 2 (over x), expert: 8 (over z, y).
Axes of the slice: x: 2, y: 2, z: 4, core: 2. Of those that a mesh axis runs over, the one named last changes fastest.
Arguments:
- tokens: bfloat16 [2, 1024, 1536], P('dp', 'expert'), may hold values from -6 to 6
- segments: int32 [2, 1024], P('dp', 'expert'), may hold values from 0 to 15, never falling along the last dimension, each value on 1 to 512 neighbouring positions
- attn_gain: bfloat16 [1536], replicated, may hold values from 0.5 to 1.5
- query_weight: bfloat16 [1536, 1536], P(None, 'section'), as said below
- key_value_weight: bfloat16 [1536, 1024], P(None, 'section'), as said below
- out_weight: bfloat16 [1536, 1536], P('section'), may hold values from -0.5 to 0.5
- ffn_gain: bfloat16 [1536], replicated, may hold values from 0.5 to 1.5
- gate_weight: bfloat16 [16, 1536, 512], P('expert', None, 'section'), may hold values from -0.15625 to 0.15625
- up_weight: bfloat16 [16, 1536, 512], P('expert', None, 'section'), may hold values from -0.15625 to 0.15625
- down_weight: bfloat16 [16, 512, 1536], P('expert', 'section'), may hold values from -0.75 to 0.75
- expert_ids: int32 [2, 1024, 8], P('dp', 'expert'), may hold values from 0 to 15, all different within a row; in each aligned block of 128 rows (0 to 127, 128 to 255, ..., all dimensions but the last counted through in order) at most 96 rows name the same one
- route_weight: float32 [2, 1024, 8], P('dp', 'expert'), may hold values from 0.1 to 1
- stream_page_table: int32 [2, 8], P('dp', 'expert'), may hold values from 0 to 15, as said below
Outputs:
- layer_out: bfloat16 [2, 1024, 1536], P('dp', 'expert', 'section')
- key_value_cache: bfloat16 [16, 128, 1024], P(('dp', 'expert'), None, 'section')
The draws below stay inside these ranges and needn't reach their ends.
Inputs may be any that keep to these rules, and one draw needn't show every extreme that they name: `stream_page_table`: every cache page is written by exactly one page of a stream; page r of a stream goes to a cache page held at expert index r, and the 1 pages held at one device go to 1 different indices of dp. `expert_ids`: the rows of one device name no expert more than 96 times; some expert is named exactly 96 times by the rows of some device. `segments`: segment ids never fall along a stream; a document spans 1 to 512 positions. `query_weight`: entries lie within -4 / sqrt(1536) and 4 / sqrt(1536). `key_value_weight`: entries lie within -160 / sqrt(1536) and 160 / sqrt(1536).
All inputs are finite; a program needn't handle non-finite values.
Results may differ from the reference program's by a relative error of at most 0.013.
The reference program's roundings to bfloat16 on the way count: a program that leaves them out, or rounds other values in their place, can miss the bound.
Values may be sent and summed in bfloat16 or wider, within the bound.
A program may use at most 128 MiB of HBM per device.

```python
import math
import jax
import jax.numpy as jnp
import numpy as np
from jax import lax

MODEL_WIDTH = 1536
QUERY_HEADS = 24
KEYVALUE_HEADS = 8
HEAD_WIDTH = 64
FF = 512
TOPK = 8
PAGE_TOKENS = 128
TOK_DEV = 128
EXPERTS = 16
STREAM_LENGTH = 1024
STREAM_PAGES = 8
PAGES_DEV = 1
TOTAL_CACHE_PAGES = 16
CAP = 96
DOCS = 16
N_DP = 2
N_EXPERT = 8


def grouped_query_rows(key):
    return jax.random.truncated_normal(jax.random.fold_in(key, 101), -4.0, 4.0, (MODEL_WIDTH, QUERY_HEADS * HEAD_WIDTH), jnp.float32) * MODEL_WIDTH ** (-0.5)


def draw_query_weight(key, part):
    return grouped_query_rows(key).astype(jnp.bfloat16)


def draw_key_value_weight(key, part):
    newest_rows = jax.random.truncated_normal(jax.random.fold_in(key, 202), -4.0, 4.0, (MODEL_WIDTH, KEYVALUE_HEADS, 2, HEAD_WIDTH), jnp.float32) * MODEL_WIDTH ** (-0.5)
    return newest_rows.reshape(MODEL_WIDTH, KEYVALUE_HEADS * 2 * HEAD_WIDTH).astype(jnp.bfloat16)


def draw_stream_page_table(key, part):
    columns = jnp.arange(N_EXPERT, dtype=jnp.int32)
    owner_order = jax.vmap(lambda column: jax.random.permutation(jax.random.fold_in(key, 1000 + column), N_DP))(columns)
    offsets = jax.vmap(lambda column: jax.random.permutation(jax.random.fold_in(key, 5000 + column), N_DP)[:PAGES_DEV])(columns)
    slot_turns = jax.random.randint(jax.random.fold_in(key, 9), (N_DP, N_EXPERT), 0, PAGES_DEV)
    holder = jnp.arange(N_DP, dtype=jnp.int32)[:, None, None]
    col_index = columns[None, :, None]
    within = jnp.arange(PAGES_DEV, dtype=jnp.int32)[None, None, :]
    owner_row = owner_order[col_index, (holder + offsets[col_index, within]) % N_DP]
    slot_index = (within + slot_turns[owner_row, col_index]) % PAGES_DEV
    return ((owner_row * N_EXPERT + col_index) * PAGES_DEV + slot_index).astype(jnp.int32).reshape(N_DP, N_EXPERT * PAGES_DEV)


def block_levels(own_key, dims, pieces, low, high):
    level = 1.0
    for dim, blocks in pieces:
        steps = jax.random.uniform(jax.random.fold_in(jax.random.fold_in(own_key, 6), dim), (blocks,), jnp.float32, low / len(pieces), high / len(pieces))
        level = level * jnp.repeat(jnp.exp(steps), dims[dim] // blocks).reshape((-1,) + (1,) * (len(dims) - 1 - dim))
    return level


def length_profile(amount, total, bound, skew):
    loads = [(1 << 20) // math.isqrt(rank ** skew) + 1 for rank in range(2, amount + 1)]
    spare, holding = total - bound - (amount - 1), [1] * (amount - 1)
    while spare > 0:
        free = [i for i in range(amount - 1) if holding[i] < bound]
        mass, remaining = sum([loads[i] for i in free]), spare
        for i in free:
            addition = min(bound - holding[i], max(1, remaining * loads[i] // mass), spare)
            holding[i] = holding[i] + addition
            spare = spare - addition
    return np.array([bound] + holding)


def ragged_sizes(rng, count, total, limit, slope):
    if count == 2:
        one = jax.random.randint(rng, (), max(1, total - limit), min(limit, total - 1) + 1)
        return jnp.stack([one, total - one])
    sizes = jnp.asarray(length_profile(count, total, limit, slope), jnp.int32)
    couples = (count - 1) // 2
    source_of, receiver = sizes[1:1 + 2 * couples:2], sizes[2:2 + 2 * couples:2]
    slack = jnp.minimum(source_of - 1, limit - receiver)
    shifted = jax.random.randint(jax.random.fold_in(rng, 1), (couples,), 0, 1 << 20) % (slack + 1)
    sizes = sizes.at[1:1 + 2 * couples:2].set(source_of - shifted).at[2:2 + 2 * couples:2].set(receiver + shifted)
    return sizes[jax.random.permutation(jax.random.fold_in(rng, 2), count)]


def deal_out(stream_key, own, number, rows, number_of, top, limit, skew):
    sequence = jax.random.permutation(stream_key, number_of)
    packed, ordinary = shares(number_of, rows * top, limit, skew, True), shares(number_of, rows * top, limit, skew, False)
    places = jnp.arange(number_of)

    def named(lengths, offset_by):
        used = int((lengths > 0).sum())
        fixed = max(1, used // 4)
        moved = fixed + (places - fixed + offset_by * (used - fixed)) % max(1, number_of - fixed)
        return jnp.zeros((number_of,), jnp.int32).at[sequence[jnp.where(places < fixed, places, moved)]].set(jnp.asarray(lengths, jnp.int32))

    lengths = jnp.where(number % 4 == 0, named(packed, number // 4), named(ordinary, number - number // 4 - 1))
    mixed = jax.random.permutation(jax.random.fold_in(own, 3), number_of)
    source_of, receiver = mixed[0:number_of // 2 * 2:2], mixed[1:number_of // 2 * 2:2]
    slack = jnp.minimum(lengths[source_of] - 1, limit - lengths[receiver]) // 2
    slack = jnp.where((source_of == sequence[0]) | (receiver == sequence[0]) | (lengths[receiver] == 0), 0, jnp.maximum(slack, 0))
    moved = jax.random.randint(jax.random.fold_in(own, 4), (number_of // 2,), 0, 1 << 20) % (slack + 1)
    lengths = lengths.at[source_of].add(-moved).at[receiver].add(moved)
    labels = jnp.searchsorted(jnp.cumsum(lengths), jnp.arange(rows * top), side="right").astype(jnp.int32)
    listing = labels.reshape(top, rows).T
    listing = listing[jax.random.permutation(jax.random.fold_in(own, 1), rows)]
    offset_by = jax.random.randint(jax.random.fold_in(own, 2), (rows, 1), 0, top)
    return jnp.take_along_axis(listing, (jnp.arange(top)[None, :] + offset_by) % top, axis=1)


def shares(count, total, limit, slope, full):
    weights = [(1 << 20) // math.isqrt(grade ** slope) + 1 for grade in range(1, count + 1)]
    largest = limit if full else min(limit, max(-(-total // count), total * weights[0] // sum(weights)))
    least = 1 if total - largest >= count - 1 else 0
    given, spare = [largest] + [least] * (count - 1), total - largest - least * (count - 1)
    while spare > 0:
        candidates = [i for i in range(1, count) if given[i] < largest] or [i for i in range(1, count) if given[i] < limit]
        pool, budget = sum([weights[i] for i in candidates]), spare
        for i in candidates:
            more = min(limit - given[i], max(1, budget * weights[i] // pool), spare)
            given[i] = given[i] + more
            spare = spare - more
    return np.array(given)


def bell_draw(stream_key, shape, scale, most, shards=(), kind=jnp.bfloat16):
    result = scale * jax.random.normal(stream_key, shape, jnp.float32)
    if shards:
        result = result * block_levels(stream_key, shape, shards, -0.22, 0.18)
    return jnp.clip(result, -most, most).astype(kind)


def setup_inputs(seed: int = 0) -> dict:
    key_list = jax.random.split(jax.random.key(seed), 14)
    tokens = bell_draw(key_list[0], (N_DP, STREAM_LENGTH, MODEL_WIDTH), 1.0, 6.0, ((0, 2), (1, 8)))
    segments = jax.vmap(lambda own: jnp.searchsorted(jnp.cumsum(ragged_sizes(own, DOCS, STREAM_LENGTH, STREAM_LENGTH // 2, 2)), jnp.arange(STREAM_LENGTH), side="right"))(jax.random.split(key_list[1], N_DP)).reshape((N_DP, STREAM_LENGTH)).astype(jnp.int32)
    attn_gain = jnp.clip(1.0 + 0.1 * jax.random.normal(key_list[2], (MODEL_WIDTH,), jnp.float32), 0.5, 1.5).astype(jnp.bfloat16)
    query_weight = draw_query_weight(jax.random.fold_in(key_list[13], 71), 0)
    key_value_weight = draw_key_value_weight(jax.random.fold_in(key_list[13], 71), 0)
    out_weight = bell_draw(key_list[5], (QUERY_HEADS * HEAD_WIDTH, MODEL_WIDTH), (2 * HEAD_WIDTH) ** -0.5, 0.5, ((0, 2),))
    ffn_gain = jnp.clip(1.0 + 0.1 * jax.random.normal(key_list[6], (MODEL_WIDTH,), jnp.float32), 0.5, 1.5).astype(jnp.bfloat16)
    gate_weight = bell_draw(key_list[7], (EXPERTS, MODEL_WIDTH, FF), MODEL_WIDTH ** -0.5, 0.15625, ((0, 8), (2, 2)))
    up_weight = bell_draw(key_list[8], (EXPERTS, MODEL_WIDTH, FF), MODEL_WIDTH ** -0.5, 0.15625, ((0, 8), (2, 2)))
    down_weight = bell_draw(key_list[9], (EXPERTS, FF, MODEL_WIDTH), (FF // 8) ** -0.5, 0.75, ((0, 8), (1, 2)))
    expert_ids_keys = jax.random.split(jax.random.fold_in(key_list[10], 1), N_DP * STREAM_LENGTH // TOK_DEV)
    expert_ids_turns = jax.random.permutation(jax.random.fold_in(key_list[10], 3), N_DP * STREAM_LENGTH // TOK_DEV)
    expert_ids = jax.vmap(lambda own, number: deal_out(jax.random.fold_in(key_list[10], 2), own, number, TOK_DEV, EXPERTS, TOPK, CAP, 1))(expert_ids_keys, expert_ids_turns).reshape((N_DP, STREAM_LENGTH, TOPK))
    route_weight = jnp.clip(jnp.exp(math.log(1.0) - 2.3025851 * jax.random.uniform(key_list[11], (N_DP, STREAM_LENGTH, TOPK), jnp.float32) ** block_levels(key_list[11], (N_DP, STREAM_LENGTH, TOPK), ((0, 2), (1, 8)), -0.2, 0.2)), 0.1, 1.0)
    stream_page_table = draw_stream_page_table(jax.random.fold_in(key_list[13], 71), 0)
    return {"tokens": tokens, "segments": segments, "attn_gain": attn_gain, "query_weight": query_weight, "key_value_weight": key_value_weight, "out_weight": out_weight, "ffn_gain": ffn_gain, "gate_weight": gate_weight, "up_weight": up_weight, "down_weight": down_weight, "expert_ids": expert_ids, "route_weight": route_weight, "stream_page_table": stream_page_table}


def rms_norm(values, norm_gain):
    return values * lax.rsqrt(lax.optimization_barrier(jnp.mean(values * values, axis=-1, keepdims=True)) + 1e-06) * norm_gain

def rotary(projected_rows, positions):
    half_dim = projected_rows.shape[-1] // 2
    frequency = 10000.0 ** (-(jnp.arange(half_dim, dtype=jnp.float32) * 2.0 / projected_rows.shape[-1]))
    angles = positions.astype(jnp.float32)[:, None] * frequency[None, :]
    cosine = jnp.cos(angles)[:, None, :]
    sine_part = jnp.sin(angles)[:, None, :]
    first_half = projected_rows[..., :half_dim]
    second = projected_rows[..., half_dim:]
    return jnp.concatenate([first_half * cosine - second * sine_part, second * cosine + first_half * sine_part], axis=-1)

def stream_layer(inputs, attn_gain, query_weight, key_value_weight, out_weight):
    stream_tokens, stream_segments = inputs
    values = stream_tokens.astype(jnp.float32)
    normalized_rows = rms_norm(values, attn_gain.astype(jnp.float32)).astype(jnp.bfloat16)
    positions = jnp.arange(STREAM_LENGTH, dtype=jnp.int32)
    query_matrix = rotary(jnp.dot(normalized_rows, query_weight, preferred_element_type=jnp.float32).reshape(STREAM_LENGTH, QUERY_HEADS, HEAD_WIDTH), positions).astype(jnp.bfloat16)
    projected_rows = jnp.dot(normalized_rows, key_value_weight, preferred_element_type=jnp.float32).reshape(STREAM_LENGTH, KEYVALUE_HEADS, 2, HEAD_WIDTH)
    key_value_rows = jnp.stack([rotary(projected_rows[:, :, 0], positions), projected_rows[:, :, 1]], axis=2).astype(jnp.bfloat16)
    key_matrix = key_value_rows[:, :, 0].astype(jnp.float32)
    value_matrix = key_value_rows[:, :, 1].astype(jnp.float32)
    query_group_width = QUERY_HEADS // KEYVALUE_HEADS
    rows_per_block = min(512, STREAM_LENGTH)

    def one_block(block_index):
        starting_row = block_index * rows_per_block
        query_block_rows = lax.dynamic_slice_in_dim(query_matrix, starting_row, rows_per_block, 0).astype(jnp.float32).reshape(rows_per_block, KEYVALUE_HEADS, query_group_width, HEAD_WIDTH)
        score_matrix = jnp.einsum('jzmx,nzx->zmjn', query_block_rows, key_matrix) / math.sqrt(HEAD_WIDTH)
        query_pos = starting_row + jnp.arange(rows_per_block, dtype=jnp.int32)
        query_seg = lax.dynamic_slice_in_dim(stream_segments, starting_row, rows_per_block, 0)
        allowed = (positions[None, :] <= query_pos[:, None]) & (stream_segments[None, :] == query_seg[:, None])
        score_matrix = jnp.where(allowed, score_matrix, -1e+30)
        row_top = lax.optimization_barrier(jnp.max(score_matrix, axis=-1, keepdims=True))
        unscaled = jnp.where(allowed, jnp.exp(score_matrix - row_top), 0.0)
        total_row_count = lax.optimization_barrier(jnp.sum(unscaled, axis=-1))
        rounded_rows = lax.optimization_barrier(unscaled.astype(jnp.bfloat16)).astype(jnp.float32)
        attention_rows = jnp.einsum('yibo,oyn->yibn', rounded_rows, value_matrix) / total_row_count[..., None]
        return attention_rows.transpose(2, 0, 1, 3).reshape(rows_per_block, QUERY_HEADS * HEAD_WIDTH).astype(jnp.bfloat16)
    attended = lax.map(one_block, jnp.arange(STREAM_LENGTH // rows_per_block, dtype=jnp.int32)).reshape(STREAM_LENGTH, QUERY_HEADS * HEAD_WIDTH)
    residual_rows = values + jnp.dot(attended, out_weight, preferred_element_type=jnp.float32)
    return (residual_rows, key_value_rows.reshape(STREAM_LENGTH, KEYVALUE_HEADS * 2 * HEAD_WIDTH))

def reference(tokens, segments, attn_gain, query_weight, key_value_weight, out_weight, ffn_gain, gate_weight, up_weight, down_weight, expert_ids, route_weight, stream_page_table):
    residual_rows, key_value_rows = lax.map(lambda paired: stream_layer(paired, attn_gain, query_weight, key_value_weight, out_weight), (tokens, segments))
    rows_per_page = key_value_rows.reshape(N_DP * STREAM_PAGES, PAGE_TOKENS, KEYVALUE_HEADS * 2 * HEAD_WIDTH)
    key_value_cache = jnp.zeros((TOTAL_CACHE_PAGES, PAGE_TOKENS, KEYVALUE_HEADS * 2 * HEAD_WIDTH), jnp.bfloat16).at[stream_page_table.reshape(-1)].set(rows_per_page)
    all_rows = N_DP * STREAM_LENGTH
    flat_resid = residual_rows.reshape(all_rows, MODEL_WIDTH)
    moe_in = rms_norm(flat_resid, ffn_gain.astype(jnp.float32)).astype(jnp.bfloat16)
    chosen_ids = expert_ids.reshape(all_rows, TOPK)
    raw_weights = route_weight.reshape(all_rows, TOPK)
    share = raw_weights / lax.optimization_barrier(jnp.sum(raw_weights, axis=1, keepdims=True))
    most_rows = N_DP * N_EXPERT * CAP
    half_units = FF // 2

    def one_expert(running, expert_data):
        expert_index, gate_mat, up_mat, down_mat = expert_data
        chosen = chosen_ids == expert_index
        hit_row = jnp.any(chosen, axis=1)
        weight_row = lax.optimization_barrier(jnp.sum(jnp.where(chosen, share, 0.0), axis=1))
        order_row = (jnp.cumsum(hit_row.astype(jnp.int32)) - 1).astype(jnp.int32)
        target_row = jnp.where(hit_row, order_row, most_rows).astype(jnp.int32)
        source_row = jnp.zeros((most_rows,), jnp.int32).at[target_row].set(jnp.arange(all_rows, dtype=jnp.int32), mode='drop')
        used_row = jnp.arange(most_rows, dtype=jnp.int32) < jnp.sum(hit_row.astype(jnp.int32))
        picked = moe_in[source_row]
        gate_out = jnp.dot(picked, gate_mat, preferred_element_type=jnp.float32)
        up_out = jnp.dot(picked, up_mat, preferred_element_type=jnp.float32)
        activ = (jax.nn.silu(gate_out) * up_out).astype(jnp.bfloat16)
        part_one = jnp.dot(activ[:, :half_units], down_mat[:half_units], preferred_element_type=jnp.float32).astype(jnp.bfloat16)
        part_two = jnp.dot(activ[:, half_units:], down_mat[half_units:], preferred_element_type=jnp.float32).astype(jnp.bfloat16)
        part_one, part_two = lax.optimization_barrier((part_one, part_two))
        expert_out = (part_one.astype(jnp.float32) + part_two.astype(jnp.float32)).astype(jnp.bfloat16)
        merged = lax.optimization_barrier(expert_out).astype(jnp.float32)
        scale_rows = jnp.where(used_row, weight_row[source_row], 0.0)
        running = running.at[source_row].add(scale_rows[:, None] * merged)
        return (running, None)
    attention_rows, unused_out = lax.scan(one_expert, jnp.zeros((all_rows, MODEL_WIDTH), jnp.float32), (jnp.arange(EXPERTS, dtype=jnp.int32), gate_weight, up_weight, down_weight))
    layer_out = (flat_resid + attention_rows).astype(jnp.bfloat16).reshape(N_DP, STREAM_LENGTH, MODEL_WIDTH)
    return (layer_out, key_value_cache)
```

```python
import functools
import math

import jax
import jax.numpy as jnp
import numpy as np
from jax import lax
from jax.experimental import pallas as pl
from jax.experimental.pallas import tpu as pltpu
from jax.sharding import PartitionSpec as P

QUERY_HEADS = 24
KEYVALUE_HEADS = 8
HEAD_WIDTH = 64
LANES = 128
EXTRA = 16
GATHER_CHUNKS = 2
MESH = pl.DeviceIdType.MESH
F32 = jnp.float32
BF16 = jnp.bfloat16


def dot(a, b):
    return jnp.dot(a, b, preferred_element_type=F32)


def layer_kernel(
    n, nd, win,
    tokens, segments, attn_gain, ffn_gain, expert_ids, route_weight, page,
    cos_hbm, sin_hbm, wq_hbm, wkv_hbm, wo_hbm, wg_hbm, wu_hbm, wd_hbm,
    out, cache,
    wq, wkv, wo, wg, wu, wd, cosv, sinv,
    tbl, rt, nrm, kvw, dpr, qs, bias, attd, hp, hps, hpr, rs, rr, mb,
    act, secs, secr, mine, ysnd, yrcv, sown, zsnd, zrcv, ns, nr, fys, fyr,
    wsem, kvzs, kvys, kvrs, dpss, dprs, hsem, rsem_r, ups, downs, yss, pss, mbrs,
    secss, secrs, yrss, yrrs, zrss, zrrs, nss, nrs, fyss, fyrs, rtss, rtrs,
):
    s = lax.axis_index("section")
    d = lax.axis_index("dp")
    c = lax.axis_index("expert")
    nz = n // 2
    z = c // 2
    y = c % 2
    T = tokens.shape[1]
    H = T // 2
    W = tokens.shape[2]
    HW = W // 2
    PW = HW // 2
    EL = wg.shape[0]
    FL = wg.shape[2]
    LKV = wkv.shape[1] // LANES
    G = QUERY_HEADS // KEYVALUE_HEADS
    ypeer = z * 2 + (1 - y)

    def local(src, dst, i):
        return pltpu.make_async_copy(src, dst, wsem.at[i])

    loads = [
        local(wkv_hbm, wkv, 0),
        local(cos_hbm.at[pl.ds(pl.multiple_of(c * T, T), T)], cosv, 1),
        local(sin_hbm.at[pl.ds(pl.multiple_of(c * T, T), T)], sinv, 2),
        local(wq_hbm, wq, 3),
        local(wo_hbm, wo, 4),
        local(wg_hbm, wg, 5),
        local(wu_hbm, wu, 6),
        local(wd_hbm, wd, 7),
    ]
    for copy in loads[:4]:
        copy.start()

    barrier = pltpu.get_barrier_semaphore()
    for k in range(1, n):
        pl.semaphore_signal(barrier, inc=1, device_id={"expert": (c + k) % n}, device_id_type=MESH)
    for k in range(1, nd):
        pl.semaphore_signal(barrier, inc=1, device_id={"dp": (d + k) % nd}, device_id_type=MESH)
    pl.semaphore_signal(barrier, inc=1, device_id={"section": 1 - s}, device_id_type=MESH)

    def remote(src, dst, ss, rsm, **dev):
        return pltpu.make_async_remote_copy(
            src_ref=src, dst_ref=dst, send_sem=ss, recv_sem=rsm, device_id=dev, device_id_type=MESH
        )

    x = tokens[0].astype(F32)
    scale = lax.rsqrt(jnp.mean(x * x, axis=-1, keepdims=True) + 1e-06)
    nrm[...] = (x * scale * attn_gain[...].astype(F32).reshape(1, W)).astype(BF16)
    lane = lax.broadcasted_iota(jnp.int32, (T, LANES), 1)
    for i in range(3):
        loads[i].wait()
    cosine = cosv[...]
    sine = sinv[...]
    key_cos = jnp.where(lane < 64, cosine, 1.0)
    key_lo = jnp.where(lane < 32, -sine, 0.0)
    key_hi = jnp.where((lane >= 32) & (lane < 64), sine, 0.0)
    for h in range(LKV):
        ch = dot(nrm[...], wkv[:, h * LANES:(h + 1) * LANES])
        ch = ch * key_cos + pltpu.roll(ch, 96, 1) * key_lo + pltpu.roll(ch, 32, 1) * key_hi
        kvw[0, 0:T, h * LANES:(h + 1) * LANES] = ch.astype(BF16)
    kvw[0, T:T + EXTRA, :] = jnp.zeros((EXTRA, kvw.shape[2]), BF16)
    seg_row = segments[...].astype(F32)
    kvw[0, T:T + EXTRA, 0:T] = jnp.broadcast_to(seg_row, (EXTRA, T)).astype(BF16)
    kvw[0, T:T + EXTRA, T:T + LANES] = jnp.broadcast_to(
        page[...].astype(F32), (EXTRA, LANES)
    ).astype(BF16)

    ids = expert_ids[0]
    raw = route_weight[0]
    share = raw / jnp.sum(raw, axis=0, keepdims=True)
    row = lax.broadcasted_iota(jnp.int32, (8, T), 0)
    for g in range(n):
        table = jnp.zeros((8, T), F32)
        for k in range(expert_ids.shape[1]):
            hit = (row < EL) & (row + g * EL == ids[k:k + 1, :])
            table = table + jnp.where(hit, share[k:k + 1, :], 0.0)
        tbl[g] = table
    rt[c] = tbl[c]

    def rt_copy(k):
        to = lax.rem(c + k, n)
        return remote(tbl.at[to], rt.at[c], rtss.at[k - 1], rtrs.at[c], expert=to)

    pl.semaphore_wait(barrier, (n - 1) + (nd - 1) + 1)

    steps = win // 2

    def kv_z(k):
        return remote(
            kvw.at[2 * k], kvw.at[2 * k + 2], kvzs.at[k], kvrs.at[2 * k + 1],
            expert=lax.rem(c + 2, n),
        )

    def kv_y(k):
        to = 2 * k + 1 - 2 * y
        return remote(kvw.at[2 * k], kvw.at[to], kvys.at[k], kvrs.at[to - 1], expert=ypeer)

    def kv_arrived(j):
        remote(kvw.at[0], kvw.at[j], kvzs.at[0], kvrs.at[j - 1], expert=ypeer).wait_recv()

    def sends_z(k):
        return (z >= k) & (z + 1 < nz) & (k < steps)

    def sends_y(k):
        if k == 0:
            return y == 0
        return (z >= k) if k < steps else (z >= k) & (y == 1)

    def kv_send(k):
        if k < steps:
            @pl.when(sends_z(k))
            def _():
                kv_z(k).start()

        @pl.when(sends_y(k))
        def _():
            kv_y(k).start()

    kv_send(0)
    for j in range(1, win + 1):
        @pl.when(c < j)
        def _():
            kvw[j] = jnp.zeros(kvw.shape[1:], BF16)

    def dp_copy(k):
        return remote(kvw.at[0], dpr.at[k - 1], dpss.at[k - 1], dprs.at[k - 1], dp=(d + k) % nd)

    for k in range(1, nd):
        dp_copy(k).start()
    for k in range(1, n):
        rt_copy(k).start()

    for copy in loads[4:]:
        copy.start()

    loads[3].wait()
    q_cos = cosine * 0.125
    q_lo = jnp.where(lane % 64 < 32, -sine, 0.0) * 0.125
    q_hi = jnp.where(lane % 64 >= 32, sine, 0.0) * 0.125
    for h2 in range(qs.shape[1] // 256):
        pair = dot(nrm[...], wq[:, h2 * 256:(h2 + 1) * 256])
        for o in range(2):
            ch = pair[:, o * LANES:(o + 1) * LANES]
            ch = ch * q_cos + pltpu.roll(ch, 96, 1) * q_lo + pltpu.roll(ch, 32, 1) * q_hi
            at = h2 * 256 + o * LANES
            qs[:, at:at + LANES] = ch.astype(BF16).astype(F32)

    my_rows = pl.ds(pl.multiple_of(s * H, H), H)
    other_rows = pl.ds(pl.multiple_of((1 - s) * H, H), H)
    def rows_of(col, sec):
        return pl.ds(pl.multiple_of((col * 2 + sec) * H, H), H)

    for k in range(1, steps + 1):
        @pl.when(z >= k)
        def _():
            kv_arrived(2 * k)
        kv_send(k)
    for k in range(steps):
        @pl.when(c >= 2 * k + 1)
        def _():
            kv_arrived(2 * k + 1)

    eye = lax.broadcasted_iota(jnp.int32, (T, T), 0)
    col = lax.broadcasted_iota(jnp.int32, (T, T), 1)
    seg_col = jnp.sum(jnp.where(eye == col, jnp.broadcast_to(seg_row, (T, T)), 0.0), axis=1, keepdims=True)
    for j in range(win + 1):
        seg_j = kvw[j, T:T + EXTRA, 0:T][0:1].astype(F32)
        key_pos = (c - j) * T + col
        allowed = (key_pos >= 0) & (key_pos <= c * T + eye) & (seg_j == seg_col)
        bias[:, j * T:(j + 1) * T] = jnp.where(allowed, 0.0, -1e30)

    heads = []
    keys = (win + 1) * T
    for zh in range(LKV):
        kv_head = kvw[:, 0:T, zh * LANES:(zh + 1) * LANES].reshape(keys, LANES)
        group = []
        for m in range(G):
            h = zh * G + m
            ch = qs[:, (h // 2) * LANES:(h // 2 + 1) * LANES]
            if h % 2:
                ch = pltpu.roll(ch, 64, 1)
            group.append(jnp.where(lane < 64, ch, 0.0).astype(BF16))
        q3 = jnp.concatenate(group, axis=0)
        score = lax.dot_general(q3, kv_head, (((1,), (1,)), ((), ())), preferred_element_type=F32)
        score = score.reshape(G, T, keys) + bias[...][None]
        top = jnp.max(score, axis=-1, keepdims=True)
        unscaled = jnp.exp(score - top)
        count = jnp.sum(unscaled, axis=-1, keepdims=True)
        weighted = dot(unscaled.astype(BF16).reshape(G * T, keys), kv_head).reshape(G, T, LANES)
        weighted = weighted / count
        for m in range(G):
            heads.append(weighted[m])
            if len(heads) == 2:
                k = (zh * G + m) // 2
                both = jnp.where(lane < 64, pltpu.roll(heads[0], 64, 1), heads[1])
                attd[:, k * LANES:(k + 1) * LANES] = both.astype(BF16)
                heads = []

    loads[4].wait()
    for k in range(W // 256):
        hp[:, k * 256:(k + 1) * 256] = dot(attd[...], wo[:, k * 256:(k + 1) * 256])
    hps[...] = hp[other_rows, :].astype(BF16)
    head_copy = remote(hps, hpr, hsem.at[0], hsem.at[1], section=1 - s)
    head_copy.start()

    for k in range(1, nd):
        dp_copy(k).wait_recv()
    target = (d * n + c).astype(F32)
    own_id = kvw[0, T:T + EXTRA, T:T + LANES][0:1, 0:1].astype(F32)
    picked = jnp.where(own_id == target, kvw[0, 0:T, :].astype(F32), 0.0)
    for k in range(1, nd):
        that_id = dpr[k - 1, T:T + EXTRA, T:T + LANES][0:1, 0:1].astype(F32)
        picked = jnp.where(that_id == target, dpr[k - 1, 0:T, :].astype(F32), picked)
    cache[0] = picked.astype(BF16)

    head_copy.wait_recv()
    resid = tokens[0, my_rows, :].astype(F32) + (hp[my_rows, :] + hpr[...].astype(F32))
    rs[...] = resid
    scale = lax.rsqrt(jnp.mean(resid * resid, axis=-1, keepdims=True) + 1e-06)
    mb[rows_of(c, s), :] = (resid * scale * ffn_gain[...].astype(F32).reshape(1, W)).astype(BF16)

    CH = GATHER_CHUNKS
    HR = H // CH

    def mb_copy(colm, sec, h, ss, **dev):
        rows = pl.ds(pl.multiple_of((colm * 2 + sec) * H + h * HR, HR), HR)
        return remote(mb.at[rows], mb.at[rows], ss, mbrs.at[(colm * 2 + sec) * CH + h], **dev)

    def up_copy(zi, h):
        return mb_copy(zi * 2 + y, s, h, ups.at[zi * CH + h], expert=lax.rem(c + 2, n))

    def down_copy(zi, h):
        return mb_copy(zi * 2 + y, s, h, downs.at[zi * CH + h], expert=lax.rem(c + n - 2, n))

    def y_copy(zi, h):
        return mb_copy(zi * 2 + y, s, h, yss.at[zi * CH + h], expert=ypeer)

    def p_copy(colm, h):
        return mb_copy(colm, s, h, pss.at[colm * CH + h], section=1 - s)

    for h in range(CH):
        @pl.when(z + 1 < nz)
        def _():
            up_copy(z, h).start()

        @pl.when(z >= 1)
        def _():
            down_copy(z, h).start()

        y_copy(z, h).start()
        p_copy(c, h).start()
    other_half = pl.ds(pl.multiple_of((1 - s) * HW, HW), HW)
    my_half = pl.ds(pl.multiple_of(s * HW, HW), HW)
    resid_copy = remote(rs.at[:, other_half], rr, rsem_r.at[0], rsem_r.at[1], section=1 - s)
    resid_copy.start()
    for i in range(5, 8):
        loads[i].wait()

    def sec_copy(i, p):
        at = 2 * i + p
        return remote(secs.at[at], secr.at[at], secss.at[at], secrs.at[at], section=1 - s)

    def yr_copy(i, p):
        at = 2 * i + p
        return remote(ysnd.at[at], yrcv.at[at], yrss.at[at], yrrs.at[at], expert=ypeer)

    def zr_copy(zi, p):
        at, to = 2 * zi + p, 2 * z + p
        return remote(zsnd.at[at], zrcv.at[to], zrss.at[at], zrrs.at[to], expert=zi * 2 + y)

    def zr_arrived(zi, p):
        at = 2 * zi + p
        remote(zsnd.at[at], zrcv.at[at], zrss.at[at], zrrs.at[at], expert=zi * 2 + y).wait_recv()

    def near(b):
        return (b == z + 1) | (b == z - 1)

    def near_copy(b, p):
        at = jnp.where(b > z, 0, 2) + p
        return remote(ns.at[at], nr.at[at], nss.at[at], nrs.at[at], expert=b * 2 + y)

    def near_arrived(at):
        remote(ns.at[at], nr.at[at], nss.at[at], nrs.at[at], expert=ypeer).wait_recv()

    def fy_copy(p):
        return remote(fys.at[p], fyr.at[p], fyss.at[p], fyrs.at[p], expert=ypeer)

    to_peer = pl.ds(pl.multiple_of((1 - y) * T, T), T)
    kept = pl.ds(pl.multiple_of(y * T, T), T)

    def layer_of(j):
        k = (j + 1) // 2
        return z + k * (1 - 2 * (j % 2))

    def exists(j):
        return (layer_of(j) >= 0) & (layer_of(j) < nz)

    def pass_on(j):
        zi = layer_of(j)

        @pl.when(exists(j) & (j < 2 * nz - 1))
        def _():
            for h in range(CH):
                mb_copy(zi * 2 + y, s, h, pss.at[0], section=1 - s).wait_recv()

                @pl.when((zi < z) & (z + 1 < nz))
                def _():
                    up_copy(zi, h).start()

                @pl.when((zi > z) & (z >= 1))
                def _():
                    down_copy(zi, h).start()

                y_copy(zi, h).start()
                p_copy(zi * 2 + y, h).start()

    pass_on(1)
    pass_on(2)
    for k in range(1, n):
        at = lax.rem(c + n - k, n)
        remote(tbl.at[0], rt.at[at], rtss.at[0], rtrs.at[at], expert=ypeer).wait_recv()

    def step(j, carry):
        @pl.when((j >= 1) & exists(j - 1) & (j - 1 < 2 * nz - 1))
        def _():
            b = layer_of(j - 1)
            for p in range(2):
                at = 2 * b + p
                sec_copy(b, p).wait_recv()

                @pl.when(b == z)
                def _():
                    mine[at] = mine[at] + secr[at].astype(F32)

                @pl.when(near(b))
                def _():
                    to = jnp.where(b > z, 0, 2) + p
                    ns[to] = (mine[at] + secr[at].astype(F32)).astype(BF16)
                    near_copy(b, p).start()

                @pl.when((b != z) & ~near(b))
                def _():
                    ysnd[at] = (mine[at, to_peer, :] + secr[at, to_peer, :].astype(F32)).astype(BF16)
                    yr_copy(b, p).start()
                    sown[at] = mine[at, kept, :] + secr[at, kept, :].astype(F32)

        pass_on(j + 3)

        @pl.when(exists(j) & (j < 2 * nz - 1))
        def _():
            zi = layer_of(j)
            theirs = zi * 2 + (1 - y)
            for h in range(CH):
                mb_copy(theirs, s, h, pss.at[0], section=1 - s).wait_recv()
                p_copy(theirs, h).start()
            for h in range(CH):
                mb_copy(zi * 2 + y, 1 - s, h, pss.at[0], section=1 - s).wait_recv()
            for h in range(CH):
                mb_copy(theirs, 1 - s, h, pss.at[0], section=1 - s).wait_recv()
            rows = pl.ds(pl.multiple_of(zi * (2 * T), 2 * T), 2 * T)
            shares = jnp.concatenate([rt[2 * zi].T, rt[2 * zi + 1].T], axis=0)
            for e in range(EL):
                share_e = shares[:, e:e + 1]
                gate = dot(mb[rows, :], wg[e])
                up = dot(mb[rows, :], wu[e])
                activ = gate / (1.0 + jnp.exp(-gate)) * up
                act[:, e * FL:(e + 1) * FL] = (activ * share_e).astype(BF16)
            for p in range(2):
                cols = pl.ds(pl.multiple_of((1 - s) * HW + p * PW, LANES), PW)
                secs[2 * zi + p] = dot(act[...], wd[:, cols]).astype(BF16)
                sec_copy(zi, p).start()
            for p in range(2):
                cols = pl.ds(pl.multiple_of(s * HW + p * PW, LANES), PW)
                mine[2 * zi + p] = dot(act[...], wd[:, cols])

        return carry

    lax.fori_loop(0, 2 * nz, step, 0)

    def far_step(j, carry):
        @pl.when(exists(j) & (j < 2 * nz - 1))
        def _():
            b = layer_of(j)
            for p in range(2):
                at = 2 * b + p
                yr_copy(b, p).wait_recv()
                zsnd[at] = (sown[at] + yrcv[at].astype(F32)).astype(BF16)
                zr_copy(b, p).start()

        return carry

    lax.fori_loop(3, min(5, 2 * nz - 1), far_step, 0)

    for p in range(2):
        for side in range(2):
            @pl.when((z >= 1) if side == 0 else (z + 1 < nz))
            def _():
                near_arrived(2 * side + p)
                mine[2 * z + p] = mine[2 * z + p] + nr[2 * side + p].astype(F32)

        fys[p] = mine[2 * z + p, to_peer, :].astype(BF16)
        fy_copy(p).start()

    lax.fori_loop(5, 2 * nz - 1, far_step, 0)
    resid_copy.wait_recv()
    for p in range(2):
        fy_copy(p).wait_recv()
        sown[2 * z + p] = mine[2 * z + p, kept, :] + fyr[p].astype(F32)

        def far_sum(k, carry):
            zi = lax.rem(z + k, nz)

            @pl.when(~near(zi))
            def _():
                zr_arrived(zi, p)
                sown[2 * z + p] = sown[2 * z + p] + zrcv[2 * zi + p].astype(F32)

            return carry

        lax.fori_loop(1, nz, far_sum, 0)
        cols = slice(p * PW, (p + 1) * PW)
        at = pl.ds(pl.multiple_of(s * HW + p * PW, LANES), PW)
        out[0, my_rows, cols] = (rs[:, at] + sown[2 * z + p, my_rows, :]).astype(BF16)
        out[0, other_rows, cols] = (rr[:, cols] + sown[2 * z + p, other_rows, :]).astype(BF16)

    for p in range(2):
        fy_copy(p).wait_send()
    for k in range(1, n):
        rt_copy(k).wait_send()

    for k in range(steps + 1):
        if k < steps:
            @pl.when(sends_z(k))
            def _():
                kv_z(k).wait_send()

        @pl.when(sends_y(k))
        def _():
            kv_y(k).wait_send()
    for k in range(1, nd):
        dp_copy(k).wait_send()
    head_copy.wait_send()
    resid_copy.wait_send()
    for zi in range(nz):
        for h in range(CH):
            @pl.when((zi <= z) & (z + 1 < nz))
            def _():
                up_copy(zi, h).wait_send()

            @pl.when((zi >= z) & (z >= 1))
            def _():
                down_copy(zi, h).wait_send()

            y_copy(zi, h).wait_send()
            p_copy(2 * zi, h).wait_send()
            p_copy(2 * zi + 1, h).wait_send()

        for p in range(2):
            @pl.when(near(zi))
            def _():
                near_copy(zi, p).wait_send()

            @pl.when((zi != z) & ~near(zi))
            def _():
                yr_copy(zi, p).wait_send()
                zr_copy(zi, p).wait_send()

        for p in range(2):
            sec_copy(zi, p).wait_send()


def trig(count):
    half = HEAD_WIDTH // 2
    frequency = np.float32(10000.0) ** (
        -(np.arange(half, dtype=np.float32) * np.float32(2.0) / np.float32(HEAD_WIDTH))
    )
    angles = np.arange(count, dtype=np.float32)[:, None] * frequency.astype(np.float32)[None, :]
    reps = LANES // half
    wide = np.tile(angles.astype(np.float64), (1, reps))
    return np.cos(wide).astype(np.float32), np.sin(wide).astype(np.float32)


def shards(
    tokens, segments, attn_gain, query_weight, key_value_weight, out_weight, ffn_gain,
    gate_weight, up_weight, down_weight, expert_ids, route_weight, stream_page_table,
):
    n = lax.axis_size("expert")
    nd = lax.axis_size("dp")
    win = n // 2
    nz = n // 2
    T, W = tokens.shape[1], tokens.shape[2]
    H, HW = T // 2, W // 2
    EL, _, FL = gate_weight.shape
    qw, kw = query_weight.shape[1], key_value_weight.shape[1]
    cosine, sine = trig(T * n)
    down = down_weight.reshape(EL * FL, W)
    vmem = pl.BlockSpec(memory_space=pltpu.VMEM)
    hbm = pl.BlockSpec(memory_space=pl.ANY)
    dma = pltpu.SemaphoreType.DMA
    out, cache = pl.pallas_call(
        functools.partial(layer_kernel, n, nd, win),
        out_shape=(
            jax.ShapeDtypeStruct((1, T, HW), BF16),
            jax.ShapeDtypeStruct((1, T, kw), BF16),
        ),
        in_specs=[vmem] * 7 + [hbm] * 8,
        out_specs=(vmem, vmem),
        scratch_shapes=[
            pltpu.VMEM((W, qw), BF16),
            pltpu.VMEM((W, kw), BF16),
            pltpu.VMEM((qw, W), BF16),
            pltpu.VMEM((EL, W, FL), BF16),
            pltpu.VMEM((EL, W, FL), BF16),
            pltpu.VMEM((EL * FL, W), BF16),
            pltpu.VMEM((T, LANES), F32),
            pltpu.VMEM((T, LANES), F32),
            pltpu.VMEM((n, 8, T), F32),
            pltpu.VMEM((n, 8, T), F32),
            pltpu.VMEM((T, W), BF16),
            pltpu.VMEM((win + 1, T + EXTRA, kw), BF16),
            pltpu.VMEM((nd - 1, T + EXTRA, kw), BF16),
            pltpu.VMEM((T, qw), F32),
            pltpu.VMEM((T, (win + 1) * T), F32),
            pltpu.VMEM((T, qw), BF16),
            pltpu.VMEM((T, W), F32),
            pltpu.VMEM((H, W), BF16),
            pltpu.VMEM((H, W), BF16),
            pltpu.VMEM((H, W), F32),
            pltpu.VMEM((H, HW), F32),
            pltpu.VMEM((n * T, W), BF16),
            pltpu.VMEM((2 * T, EL * FL), BF16),
            pltpu.VMEM((2 * nz, 2 * T, HW // 2), BF16),
            pltpu.VMEM((2 * nz, 2 * T, HW // 2), BF16),
            pltpu.VMEM((2 * nz, 2 * T, HW // 2), F32),
            pltpu.VMEM((2 * nz, T, HW // 2), BF16),
            pltpu.VMEM((2 * nz, T, HW // 2), BF16),
            pltpu.VMEM((2 * nz, T, HW // 2), F32),
            pltpu.VMEM((2 * nz, T, HW // 2), BF16),
            pltpu.VMEM((2 * nz, T, HW // 2), BF16),
            pltpu.VMEM((4, 2 * T, HW // 2), BF16),
            pltpu.VMEM((4, 2 * T, HW // 2), BF16),
            pltpu.VMEM((2, T, HW // 2), BF16),
            pltpu.VMEM((2, T, HW // 2), BF16),
            dma((8,)),
            dma((win // 2,)), dma((win // 2 + 1,)), dma((win,)),
            dma((nd - 1,)), dma((nd - 1,)),
            dma((2,)), dma((2,)),
            dma((nz * GATHER_CHUNKS,)), dma((nz * GATHER_CHUNKS,)), dma((nz * GATHER_CHUNKS,)),
            dma((n * GATHER_CHUNKS,)), dma((2 * n * GATHER_CHUNKS,)),
            dma((n,)), dma((n,)), dma((n,)), dma((n,)), dma((n,)), dma((n,)),
            dma((4,)), dma((4,)), dma((2,)), dma((2,)), dma((n,)), dma((n,)),
        ],
        compiler_params=pltpu.CompilerParams(
            collective_id=0, has_side_effects=True, vmem_limit_bytes=58 * 1024 * 1024
        ),
    )(
        tokens, segments, attn_gain, ffn_gain, expert_ids.transpose(0, 2, 1),
        route_weight.transpose(0, 2, 1), stream_page_table, jnp.asarray(cosine), jnp.asarray(sine),
        query_weight, key_value_weight, out_weight, gate_weight, up_weight, down,
    )

    def hand_over(out_in, cache_in, out_to, cache_to):
        out_to[...] = out_in[...]
        cache_to[...] = cache_in[...]

    return pl.pallas_call(
        hand_over,
        out_shape=(jax.ShapeDtypeStruct(out.shape, BF16), jax.ShapeDtypeStruct(cache.shape, BF16)),
        in_specs=[vmem, vmem],
        out_specs=(vmem, vmem),
    )(out, cache)


def solution(mesh):
    in_specs = (
        P("dp", "expert", None),
        P("dp", "expert"),
        P(),
        P(None, "section"),
        P(None, "section"),
        P("section", None),
        P(),
        P("expert", None, "section"),
        P("expert", None, "section"),
        P("expert", "section", None),
        P("dp", "expert", None),
        P("dp", "expert", None),
        P("dp", "expert"),
    )
    out_specs = (P("dp", "expert", "section"), P(("dp", "expert"), None, "section"))
    return jax.shard_map(shards, mesh=mesh, in_specs=in_specs, out_specs=out_specs, check_vma=False)
```

```python
import functools
import math

import jax
import jax.numpy as jnp
import numpy as np
from jax import lax
from jax.experimental import pallas as pl
from jax.experimental.pallas import tpu as pltpu
from jax.sharding import PartitionSpec as P

QUERY_HEADS = 24
KEYVALUE_HEADS = 8
HEAD_WIDTH = 64
LANES = 128
GATHER_CHUNKS = 2
MESH = pl.DeviceIdType.MESH
F32 = jnp.float32
BF16 = jnp.bfloat16


def dot(a, b):
    return jnp.dot(a, b, preferred_element_type=F32)


def layer_kernel(
    n, nd, win,
    tokens, segments, attn_gain, ffn_gain, expert_ids, route_weight, page,
    cos_hbm, sin_hbm, wq_hbm, wkv_hbm, wo_hbm, wg_hbm, wu_hbm, wd_hbm,
    out, cache,
    wq, wkv, wo, wg, wu, wd, cosv, sinv,
    tbl, rt, nrm, kvw, dpr, pgw, pgr, qs, bias, attd, hp, hps, hpr, rs, rr, mb,
    act, secs, secr, mine, ysnd, yrcv, sown, zsnd, zrcv, ns, nr, fys, fyr,
    wsem, kvzs, kvys, kvrs, dpss, dprs, pgss, pgrs, hsem, rsem_r, ups, downs, yss, pss, mbrs,
    secss, secrs, yrss, yrrs, zrss, zrrs, nss, nrs, fyss, fyrs, rtss, rtrs,
):
    s = lax.axis_index("section")
    d = lax.axis_index("dp")
    c = lax.axis_index("expert")
    nz = n // 2
    z = c // 2
    y = c % 2
    T = tokens.shape[1]
    H = T // 2
    W = tokens.shape[2]
    HW = W // 2
    PW = HW // 2
    EL = wg.shape[0]
    FL = wg.shape[2]
    LKV = wkv.shape[1] // LANES
    G = QUERY_HEADS // KEYVALUE_HEADS
    ypeer = z * 2 + (1 - y)

    def local(src, dst, i):
        return pltpu.make_async_copy(src, dst, wsem.at[i])

    loads = [
        local(wkv_hbm, wkv, 0),
        local(cos_hbm.at[pl.ds(pl.multiple_of(c * T, T), T)], cosv, 1),
        local(sin_hbm.at[pl.ds(pl.multiple_of(c * T, T), T)], sinv, 2),
        local(wq_hbm, wq, 3),
        local(wo_hbm, wo, 4),
        local(wg_hbm, wg, 5),
        local(wu_hbm, wu, 6),
        local(wd_hbm, wd, 7),
    ]
    for copy in loads[:4]:
        copy.start()

    barrier = pltpu.get_barrier_semaphore()
    for k in range(1, n):
        pl.semaphore_signal(barrier, inc=1, device_id={"expert": (c + k) % n}, device_id_type=MESH)
    for k in range(1, nd):
        pl.semaphore_signal(barrier, inc=1, device_id={"dp": (d + k) % nd}, device_id_type=MESH)
    pl.semaphore_signal(barrier, inc=1, device_id={"section": 1 - s}, device_id_type=MESH)

    def remote(src, dst, ss, rsm, **dev):
        return pltpu.make_async_remote_copy(
            src_ref=src, dst_ref=dst, send_sem=ss, recv_sem=rsm, device_id=dev, device_id_type=MESH
        )

    seg_row = segments[...].astype(F32)
    ids = expert_ids[0]
    raw = route_weight[0]
    share = raw / jnp.sum(raw, axis=0, keepdims=True)
    row = lax.broadcasted_iota(jnp.int32, (8, T), 0)
    for g in range(n):
        table = jnp.zeros((8, T), F32)
        for k in range(expert_ids.shape[1]):
            hit = (row < EL) & (row + g * EL == ids[k:k + 1, :])
            table = table + jnp.where(hit, share[k:k + 1, :], 0.0)
        tbl[g] = jnp.where(row == 7, seg_row, table)
    def rt_copy(k):
        to = lax.rem(c + k, n)
        return remote(tbl.at[to], rt.at[c], rtss.at[k - 1], rtrs.at[c], expert=to)

    x = tokens[0].astype(F32)
    scale = lax.rsqrt(jnp.mean(x * x, axis=-1, keepdims=True) + 1e-06)
    nrm[...] = (x * scale * attn_gain[...].astype(F32).reshape(1, W)).astype(BF16)
    lane = lax.broadcasted_iota(jnp.int32, (T, LANES), 1)
    for i in range(3):
        loads[i].wait()
    cosine = cosv[...]
    sine = sinv[...]
    key_cos = jnp.where(lane < 64, cosine, 1.0)
    key_lo = jnp.where(lane < 32, -sine, 0.0)
    key_hi = jnp.where((lane >= 32) & (lane < 64), sine, 0.0)
    pgw[...] = jnp.broadcast_to(page[...].astype(F32), pgw.shape)
    pl.semaphore_wait(barrier, (n - 1) + (nd - 1) + 1)

    steps = win // 2

    def kv_z(k, h):
        at = 2 * k + 2
        return remote(
            kvw.at[2 * k, h], kvw.at[at, h], kvzs.at[k * LKV + h], kvrs.at[(at - 1) * LKV + h],
            expert=lax.rem(c + 2, n),
        )

    def kv_y(k, h):
        to = 2 * k + 1 - 2 * y
        return remote(
            kvw.at[2 * k, h], kvw.at[to, h], kvys.at[k * LKV + h], kvrs.at[(to - 1) * LKV + h],
            expert=ypeer,
        )

    def kv_arrived(j, h):
        remote(
            kvw.at[0, h], kvw.at[j, h], kvzs.at[0], kvrs.at[(j - 1) * LKV + h], expert=ypeer
        ).wait_recv()

    def sends_z(k):
        return (z >= k) & (z + 1 < nz) & (k < steps)

    def sends_y(k):
        if k == 0:
            return y == 0
        return (z >= k) if k < steps else (z >= k) & (y == 1)

    def kv_send(k, h):
        if k < steps:
            @pl.when(sends_z(k))
            def _():
                kv_z(k, h).start()

        @pl.when(sends_y(k))
        def _():
            kv_y(k, h).start()

    for k in range(1, n):
        rt_copy(k).start()
    rt[c] = tbl[c]
    for h2 in range(LKV // 2):
        pair = dot(nrm[...], wkv[:, h2 * 256:(h2 + 1) * 256])
        for o in range(2):
            ch = pair[:, o * LANES:(o + 1) * LANES]
            ch = ch * key_cos + pltpu.roll(ch, 96, 1) * key_lo + pltpu.roll(ch, 32, 1) * key_hi
            kvw[0, 2 * h2 + o] = ch.astype(BF16)
            kv_send(0, 2 * h2 + o)
    for j in range(1, win + 1):
        @pl.when(c < j)
        def _():
            kvw[j] = jnp.zeros(kvw.shape[1:], BF16)

    def dp_copy(k):
        return remote(kvw.at[0], dpr.at[k - 1], dpss.at[k - 1], dprs.at[k - 1], dp=(d + k) % nd)

    def pg_copy(k):
        return remote(pgw, pgr.at[k - 1], pgss.at[k - 1], pgrs.at[k - 1], dp=(d + k) % nd)

    for k in range(1, nd):
        dp_copy(k).start()
        pg_copy(k).start()

    for copy in loads[4:]:
        copy.start()

    loads[3].wait()
    q_cos = cosine * 0.125
    q_lo = jnp.where(lane % 64 < 32, -sine, 0.0) * 0.125
    q_hi = jnp.where(lane % 64 >= 32, sine, 0.0) * 0.125
    for h2 in range(qs.shape[1] // 256):
        pair = dot(nrm[...], wq[:, h2 * 256:(h2 + 1) * 256])
        for o in range(2):
            ch = pair[:, o * LANES:(o + 1) * LANES]
            ch = ch * q_cos + pltpu.roll(ch, 96, 1) * q_lo + pltpu.roll(ch, 32, 1) * q_hi
            at = h2 * 256 + o * LANES
            qs[:, at:at + LANES] = ch.astype(BF16).astype(F32)

    my_rows = pl.ds(pl.multiple_of(s * H, H), H)
    other_rows = pl.ds(pl.multiple_of((1 - s) * H, H), H)
    def rows_of(col, sec):
        return pl.ds(pl.multiple_of((col * 2 + sec) * H, H), H)

    def kv_pass(k, h):
        @pl.when(z >= k)
        def _():
            kv_arrived(2 * k, h)
        kv_send(k, h)

    for k in range(1, steps):
        for h in range(LKV):
            kv_pass(k, h)
    kv_pass(steps, 0)

    def rt_arrived(at):
        remote(tbl.at[0], rt.at[at], rtss.at[0], rtrs.at[at], expert=ypeer).wait_recv()

    for k in range(1, win + 1):
        @pl.when(c >= k)
        def _():
            rt_arrived(c - k)

    eye = lax.broadcasted_iota(jnp.int32, (T, T), 0)
    col = lax.broadcasted_iota(jnp.int32, (T, T), 1)
    seg_col = jnp.sum(jnp.where(eye == col, jnp.broadcast_to(seg_row, (T, T)), 0.0), axis=1, keepdims=True)
    for j in range(win + 1):
        seg_j = rt[jnp.where(c >= j, c - j, c), 7:8, :]
        key_pos = (c - j) * T + col
        allowed = (key_pos >= 0) & (key_pos <= c * T + eye) & (seg_j == seg_col)
        bias[:, j * T:(j + 1) * T] = jnp.where(allowed, 0.0, -1e30)

    heads = []
    keys = (win + 1) * T
    for zh in range(LKV):
        if zh + 1 < LKV:
            kv_pass(steps, zh + 1)
        for k in range(steps):
            @pl.when(c >= 2 * k + 1)
            def _():
                kv_arrived(2 * k + 1, zh)
        kv_head = kvw[:, zh].reshape(keys, LANES)
        group = []
        for m in range(G):
            h = zh * G + m
            ch = qs[:, (h // 2) * LANES:(h // 2 + 1) * LANES]
            if h % 2:
                ch = pltpu.roll(ch, 64, 1)
            group.append(jnp.where(lane < 64, ch, 0.0).astype(BF16))
        q3 = jnp.concatenate(group, axis=0)
        score = lax.dot_general(q3, kv_head, (((1,), (1,)), ((), ())), preferred_element_type=F32)
        score = score.reshape(G, T, keys) + bias[...][None]
        top = jnp.max(score, axis=-1, keepdims=True)
        unscaled = jnp.exp(score - top)
        count = jnp.sum(unscaled, axis=-1, keepdims=True)
        weighted = dot(unscaled.astype(BF16).reshape(G * T, keys), kv_head).reshape(G, T, LANES)
        weighted = weighted / count
        for m in range(G):
            heads.append(weighted[m])
            if len(heads) == 2:
                k = (zh * G + m) // 2
                both = jnp.where(lane < 64, pltpu.roll(heads[0], 64, 1), heads[1])
                attd[:, k * LANES:(k + 1) * LANES] = both.astype(BF16)
                heads = []

    loads[4].wait()
    for k in range(W // 256):
        hp[:, k * 256:(k + 1) * 256] = dot(attd[...], wo[:, k * 256:(k + 1) * 256])
    hps[...] = hp[other_rows, :].astype(BF16)
    head_copy = remote(hps, hpr, hsem.at[0], hsem.at[1], section=1 - s)
    head_copy.start()

    for k in range(1, nd):
        dp_copy(k).wait_recv()
        pg_copy(k).wait_recv()
    target = (d * n + c).astype(F32)
    own_id = pgw[0:1, 0:1]
    for h in range(LKV):
        picked = jnp.where(own_id == target, kvw[0, h].astype(F32), 0.0)
        for k in range(1, nd):
            picked = jnp.where(pgr[k - 1, 0:1, 0:1] == target, dpr[k - 1, h].astype(F32), picked)
        cache[0, :, h * LANES:(h + 1) * LANES] = picked.astype(BF16)

    head_copy.wait_recv()
    resid = tokens[0, my_rows, :].astype(F32) + (hp[my_rows, :] + hpr[...].astype(F32))
    rs[...] = resid
    scale = lax.rsqrt(jnp.mean(resid * resid, axis=-1, keepdims=True) + 1e-06)
    mb[rows_of(c, s), :] = (resid * scale * ffn_gain[...].astype(F32).reshape(1, W)).astype(BF16)

    CH = GATHER_CHUNKS
    HR = H // CH

    def mb_copy(colm, sec, h, ss, **dev):
        rows = pl.ds(pl.multiple_of((colm * 2 + sec) * H + h * HR, HR), HR)
        return remote(mb.at[rows], mb.at[rows], ss, mbrs.at[(colm * 2 + sec) * CH + h], **dev)

    def up_copy(zi, h):
        return mb_copy(zi * 2 + y, s, h, ups.at[zi * CH + h], expert=lax.rem(c + 2, n))

    def down_copy(zi, h):
        return mb_copy(zi * 2 + y, s, h, downs.at[zi * CH + h], expert=lax.rem(c + n - 2, n))

    def y_copy(zi, h):
        return mb_copy(zi * 2 + y, s, h, yss.at[zi * CH + h], expert=ypeer)

    def p_copy(colm, h):
        return mb_copy(colm, s, h, pss.at[colm * CH + h], section=1 - s)

    for h in range(CH):
        @pl.when(z + 1 < nz)
        def _():
            up_copy(z, h).start()

        @pl.when(z >= 1)
        def _():
            down_copy(z, h).start()

        if h < CH // 2:
            y_copy(z, h).start()
        p_copy(c, h).start()
    other_half = pl.ds(pl.multiple_of((1 - s) * HW, HW), HW)
    my_half = pl.ds(pl.multiple_of(s * HW, HW), HW)
    resid_copy = remote(rs.at[:, other_half], rr, rsem_r.at[0], rsem_r.at[1], section=1 - s)
    resid_copy.start()
    for i in range(5, 8):
        loads[i].wait()

    def sec_copy(i, p):
        at = 2 * i + p
        return remote(secs.at[at], secr.at[at], secss.at[at], secrs.at[at], section=1 - s)

    def yr_copy(i, p):
        at = 2 * i + p
        return remote(ysnd.at[at], yrcv.at[at], yrss.at[at], yrrs.at[at], expert=ypeer)

    def zr_copy(zi, p):
        at, to = 2 * zi + p, 2 * z + p
        return remote(zsnd.at[at], zrcv.at[to], zrss.at[at], zrrs.at[to], expert=zi * 2 + y)

    def zr_arrived(zi, p):
        at = 2 * zi + p
        remote(zsnd.at[at], zrcv.at[at], zrss.at[at], zrrs.at[at], expert=zi * 2 + y).wait_recv()

    def near(b):
        return (b == z + 1) | (b == z - 1)

    def near_copy(b, p):
        at = jnp.where(b > z, 0, 2) + p
        return remote(ns.at[at], nr.at[at], nss.at[at], nrs.at[at], expert=b * 2 + y)

    def near_arrived(at):
        remote(ns.at[at], nr.at[at], nss.at[at], nrs.at[at], expert=ypeer).wait_recv()

    def fy_copy(p):
        return remote(fys.at[p], fyr.at[p], fyss.at[p], fyrs.at[p], expert=ypeer)

    to_peer = pl.ds(pl.multiple_of((1 - y) * T, T), T)
    kept = pl.ds(pl.multiple_of(y * T, T), T)

    def layer_of(j):
        k = (j + 1) // 2
        return z + k * (1 - 2 * (j % 2))

    def exists(j):
        return (layer_of(j) >= 0) & (layer_of(j) < nz)

    def pass_on(j):
        zi = layer_of(j)

        @pl.when(exists(j) & (j < 2 * nz - 1))
        def _():
            for h in range(CH):
                mb_copy(zi * 2 + y, s, h, pss.at[0], section=1 - s).wait_recv()

                @pl.when((zi < z) & (z + 1 < nz))
                def _():
                    up_copy(zi, h).start()

                @pl.when((zi > z) & (z >= 1))
                def _():
                    down_copy(zi, h).start()

                y_copy(zi, h).start()
                p_copy(zi * 2 + y, h).start()

    pass_on(1)
    pass_on(2)
    for j in range(3, min(5, 2 * nz - 1)):
        pass_on(j)
    for h in range(CH // 2, CH):
        y_copy(z, h).start()
    for k in range(1, n):
        @pl.when((c < k) | (k > win))
        def _():
            rt_arrived(lax.rem(c + n - k, n))

    def step(turn, carry):
        j = lax.rem(turn + 1, 2 * nz - 1)

        @pl.when(exists(j))
        def _():
            zi = layer_of(j)
            theirs = zi * 2 + (1 - y)
            for h in range(CH):
                mb_copy(theirs, s, h, pss.at[0], section=1 - s).wait_recv()
                p_copy(theirs, h).start()
            for h in range(CH):
                mb_copy(zi * 2 + y, 1 - s, h, pss.at[0], section=1 - s).wait_recv()
            for h in range(CH):
                mb_copy(theirs, 1 - s, h, pss.at[0], section=1 - s).wait_recv()
            rows = pl.ds(pl.multiple_of(zi * (2 * T), 2 * T), 2 * T)
            shares = jnp.concatenate([rt[2 * zi].T, rt[2 * zi + 1].T], axis=0)
            for e in range(EL):
                share_e = shares[:, e:e + 1]
                gate = dot(mb[rows, :], wg[e])
                up = dot(mb[rows, :], wu[e])
                activ = gate / (1.0 + jnp.exp(-gate)) * up
                act[:, e * FL:(e + 1) * FL] = (activ * share_e).astype(BF16)
            for p in range(2):
                cols = pl.ds(pl.multiple_of((1 - s) * HW + p * PW, LANES), PW)
                secs[2 * zi + p] = dot(act[...], wd[:, cols]).astype(BF16)
                sec_copy(zi, p).start()
            for p in range(2):
                cols = pl.ds(pl.multiple_of(s * HW + p * PW, LANES), PW)
                mine[2 * zi + p] = dot(act[...], wd[:, cols])

        @pl.when(exists(j))
        def _():
            b = layer_of(j)
            for p in range(2):
                at = 2 * b + p
                sec_copy(b, p).wait_recv()

                @pl.when(b == z)
                def _():
                    mine[at] = mine[at] + secr[at].astype(F32)

                @pl.when(near(b))
                def _():
                    to = jnp.where(b > z, 0, 2) + p
                    ns[to] = (mine[at] + secr[at].astype(F32)).astype(BF16)
                    near_copy(b, p).start()

                @pl.when((b != z) & ~near(b))
                def _():
                    ysnd[at] = (mine[at, to_peer, :] + secr[at, to_peer, :].astype(F32)).astype(BF16)
                    yr_copy(b, p).start()
                    sown[at] = mine[at, kept, :] + secr[at, kept, :].astype(F32)

        pass_on(turn + 5)
        return carry

    lax.fori_loop(0, 2 * nz - 1, step, 0)

    def far_step(j, carry):
        @pl.when(exists(j) & (j < 2 * nz - 1))
        def _():
            b = layer_of(j)
            for p in range(2):
                at = 2 * b + p
                yr_copy(b, p).wait_recv()
                zsnd[at] = (sown[at] + yrcv[at].astype(F32)).astype(BF16)
                zr_copy(b, p).start()

        return carry

    lax.fori_loop(3, min(5, 2 * nz - 1), far_step, 0)

    for p in range(2):
        for side in range(2):
            @pl.when((z >= 1) if side == 0 else (z + 1 < nz))
            def _():
                near_arrived(2 * side + p)
                mine[2 * z + p] = mine[2 * z + p] + nr[2 * side + p].astype(F32)

        fys[p] = mine[2 * z + p, to_peer, :].astype(BF16)
        fy_copy(p).start()

    lax.fori_loop(5, 2 * nz - 1, far_step, 0)
    resid_copy.wait_recv()
    for p in range(2):
        fy_copy(p).wait_recv()
        sown[2 * z + p] = mine[2 * z + p, kept, :] + fyr[p].astype(F32)

        def far_sum(k, carry):
            zi = lax.rem(z + k, nz)

            @pl.when(~near(zi))
            def _():
                zr_arrived(zi, p)
                sown[2 * z + p] = sown[2 * z + p] + zrcv[2 * zi + p].astype(F32)

            return carry

        lax.fori_loop(1, nz, far_sum, 0)
        cols = slice(p * PW, (p + 1) * PW)
        at = pl.ds(pl.multiple_of(s * HW + p * PW, LANES), PW)
        out[0, my_rows, cols] = (rs[:, at] + sown[2 * z + p, my_rows, :]).astype(BF16)
        out[0, other_rows, cols] = (rr[:, cols] + sown[2 * z + p, other_rows, :]).astype(BF16)

    for p in range(2):
        fy_copy(p).wait_send()
    for k in range(1, n):
        rt_copy(k).wait_send()

    for h in range(LKV):
        for k in range(steps + 1):
            if k < steps:
                @pl.when(sends_z(k))
                def _():
                    kv_z(k, h).wait_send()

            @pl.when(sends_y(k))
            def _():
                kv_y(k, h).wait_send()
    for k in range(1, nd):
        dp_copy(k).wait_send()
        pg_copy(k).wait_send()
    head_copy.wait_send()
    resid_copy.wait_send()
    for zi in range(nz):
        for h in range(CH):
            @pl.when((zi <= z) & (z + 1 < nz))
            def _():
                up_copy(zi, h).wait_send()

            @pl.when((zi >= z) & (z >= 1))
            def _():
                down_copy(zi, h).wait_send()

            y_copy(zi, h).wait_send()
            p_copy(2 * zi, h).wait_send()
            p_copy(2 * zi + 1, h).wait_send()

        for p in range(2):
            @pl.when(near(zi))
            def _():
                near_copy(zi, p).wait_send()

            @pl.when((zi != z) & ~near(zi))
            def _():
                yr_copy(zi, p).wait_send()
                zr_copy(zi, p).wait_send()

        for p in range(2):
            sec_copy(zi, p).wait_send()


def trig(count):
    half = HEAD_WIDTH // 2
    frequency = np.float32(10000.0) ** (
        -(np.arange(half, dtype=np.float32) * np.float32(2.0) / np.float32(HEAD_WIDTH))
    )
    angles = np.arange(count, dtype=np.float32)[:, None] * frequency.astype(np.float32)[None, :]
    reps = LANES // half
    wide = np.tile(angles.astype(np.float64), (1, reps))
    return np.cos(wide).astype(np.float32), np.sin(wide).astype(np.float32)


def shards(
    tokens, segments, attn_gain, query_weight, key_value_weight, out_weight, ffn_gain,
    gate_weight, up_weight, down_weight, expert_ids, route_weight, stream_page_table,
):
    n = lax.axis_size("expert")
    nd = lax.axis_size("dp")
    win = n // 2
    nz = n // 2
    T, W = tokens.shape[1], tokens.shape[2]
    H, HW = T // 2, W // 2
    EL, _, FL = gate_weight.shape
    qw, kw = query_weight.shape[1], key_value_weight.shape[1]
    cosine, sine = trig(T * n)
    down = down_weight.reshape(EL * FL, W)
    vmem = pl.BlockSpec(memory_space=pltpu.VMEM)
    hbm = pl.BlockSpec(memory_space=pl.ANY)
    dma = pltpu.SemaphoreType.DMA
    out, cache = pl.pallas_call(
        functools.partial(layer_kernel, n, nd, win),
        out_shape=(
            jax.ShapeDtypeStruct((1, T, HW), BF16),
            jax.ShapeDtypeStruct((1, T, kw), BF16),
        ),
        in_specs=[vmem] * 7 + [hbm] * 8,
        out_specs=(vmem, vmem),
        scratch_shapes=[
            pltpu.VMEM((W, qw), BF16),
            pltpu.VMEM((W, kw), BF16),
            pltpu.VMEM((qw, W), BF16),
            pltpu.VMEM((EL, W, FL), BF16),
            pltpu.VMEM((EL, W, FL), BF16),
            pltpu.VMEM((EL * FL, W), BF16),
            pltpu.VMEM((T, LANES), F32),
            pltpu.VMEM((T, LANES), F32),
            pltpu.VMEM((n, 8, T), F32),
            pltpu.VMEM((n, 8, T), F32),
            pltpu.VMEM((T, W), BF16),
            pltpu.VMEM((win + 1, kw // LANES, T, LANES), BF16),
            pltpu.VMEM((nd - 1, kw // LANES, T, LANES), BF16),
            pltpu.VMEM((8, LANES), F32),
            pltpu.VMEM((nd - 1, 8, LANES), F32),
            pltpu.VMEM((T, qw), F32),
            pltpu.VMEM((T, (win + 1) * T), F32),
            pltpu.VMEM((T, qw), BF16),
            pltpu.VMEM((T, W), F32),
            pltpu.VMEM((H, W), BF16),
            pltpu.VMEM((H, W), BF16),
            pltpu.VMEM((H, W), F32),
            pltpu.VMEM((H, HW), F32),
            pltpu.VMEM((n * T, W), BF16),
            pltpu.VMEM((2 * T, EL * FL), BF16),
            pltpu.VMEM((2 * nz, 2 * T, HW // 2), BF16),
            pltpu.VMEM((2 * nz, 2 * T, HW // 2), BF16),
            pltpu.VMEM((2 * nz, 2 * T, HW // 2), F32),
            pltpu.VMEM((2 * nz, T, HW // 2), BF16),
            pltpu.VMEM((2 * nz, T, HW // 2), BF16),
            pltpu.VMEM((2 * nz, T, HW // 2), F32),
            pltpu.VMEM((2 * nz, T, HW // 2), BF16),
            pltpu.VMEM((2 * nz, T, HW // 2), BF16),
            pltpu.VMEM((4, 2 * T, HW // 2), BF16),
            pltpu.VMEM((4, 2 * T, HW // 2), BF16),
            pltpu.VMEM((2, T, HW // 2), BF16),
            pltpu.VMEM((2, T, HW // 2), BF16),
            dma((8,)),
            dma((win // 2 * (kw // LANES),)), dma(((win // 2 + 1) * (kw // LANES),)), dma((win * (kw // LANES),)),
            dma((nd - 1,)), dma((nd - 1,)), dma((nd - 1,)), dma((nd - 1,)),
            dma((2,)), dma((2,)),
            dma((nz * GATHER_CHUNKS,)), dma((nz * GATHER_CHUNKS,)), dma((nz * GATHER_CHUNKS,)),
            dma((n * GATHER_CHUNKS,)), dma((2 * n * GATHER_CHUNKS,)),
            dma((n,)), dma((n,)), dma((n,)), dma((n,)), dma((n,)), dma((n,)),
            dma((4,)), dma((4,)), dma((2,)), dma((2,)), dma((n,)), dma((n,)),
        ],
        compiler_params=pltpu.CompilerParams(
            collective_id=0, has_side_effects=True, vmem_limit_bytes=58 * 1024 * 1024
        ),
    )(
        tokens, segments, attn_gain, ffn_gain, expert_ids.transpose(0, 2, 1),
        route_weight.transpose(0, 2, 1), stream_page_table, jnp.asarray(cosine), jnp.asarray(sine),
        query_weight, key_value_weight, out_weight, gate_weight, up_weight, down,
    )

    def hand_over(out_in, cache_in, out_to, cache_to):
        out_to[...] = out_in[...]
        cache_to[...] = cache_in[...]

    return pl.pallas_call(
        hand_over,
        out_shape=(jax.ShapeDtypeStruct(out.shape, BF16), jax.ShapeDtypeStruct(cache.shape, BF16)),
        in_specs=[vmem, vmem],
        out_specs=(vmem, vmem),
    )(out, cache)


def solution(mesh):
    in_specs = (
        P("dp", "expert", None),
        P("dp", "expert"),
        P(),
        P(None, "section"),
        P(None, "section"),
        P("section", None),
        P(),
        P("expert", None, "section"),
        P("expert", None, "section"),
        P("expert", "section", None),
        P("dp", "expert", None),
        P("dp", "expert", None),
        P("dp", "expert"),
    )
    out_specs = (P("dp", "expert", "section"), P(("dp", "expert"), None, "section"))
    return jax.shard_map(shards, mesh=mesh, in_specs=in_specs, out_specs=out_specs, check_vma=False)
```

```python
import functools
import math

import jax
import jax.numpy as jnp
import numpy as np
from jax import lax
from jax.experimental import pallas as pl
from jax.experimental.pallas import tpu as pltpu
from jax.sharding import PartitionSpec as P

QUERY_HEADS = 24
KEYVALUE_HEADS = 8
HEAD_WIDTH = 64
LANES = 128
GATHER_CHUNKS = 2
MESH = pl.DeviceIdType.MESH
F32 = jnp.float32
BF16 = jnp.bfloat16


def dot(a, b):
    return jnp.dot(a, b, preferred_element_type=F32)


def layer_kernel(
    n, nd, win,
    tokens, segments, attn_gain, ffn_gain, expert_ids, route_weight, page,
    cos_hbm, sin_hbm, wq_hbm, wkv_hbm, wo_hbm, wg_hbm, wu_hbm, wd_hbm,
    out, cache,
    wq, wkv, wo, wg, wu, wd, cosv, sinv,
    tbl, rt, nrm, kvw, dpr, pgw, pgr, qs, bias, attd, hp, hps, hpr, rs, rr, mb,
    act, secs, secr, mine, ysnd, yrcv, sown, zsnd, zrcv, ns, nr, fys, fyr,
    wsem, kvzs, kvys, kvrs, dpss, dprs, pgss, pgrs, hsem, rsem_r, ups, downs, yss, pss, mbrs,
    secss, secrs, yrss, yrrs, zrss, zrrs, nss, nrs, fyss, fyrs, rtss, rtrs,
):
    s = lax.axis_index("section")
    d = lax.axis_index("dp")
    c = lax.axis_index("expert")
    nz = n // 2
    z = c // 2
    y = c % 2
    T = tokens.shape[1]
    H = T // 2
    W = tokens.shape[2]
    HW = W // 2
    PW = HW // 2
    EL = wg.shape[0]
    FL = wg.shape[2]
    LKV = wkv.shape[1] // LANES
    G = QUERY_HEADS // KEYVALUE_HEADS
    ypeer = z * 2 + (1 - y)

    def local(src, dst, i):
        return pltpu.make_async_copy(src, dst, wsem.at[i])

    loads = [
        local(wkv_hbm, wkv, 0),
        local(cos_hbm.at[pl.ds(pl.multiple_of(c * T, T), T)], cosv, 1),
        local(sin_hbm.at[pl.ds(pl.multiple_of(c * T, T), T)], sinv, 2),
        local(wq_hbm, wq, 3),
        local(wo_hbm, wo, 4),
        local(wg_hbm, wg, 5),
        local(wu_hbm, wu, 6),
        local(wd_hbm, wd, 7),
    ]
    for copy in loads[:4]:
        copy.start()

    barrier = pltpu.get_barrier_semaphore()
    for k in range(1, n):
        pl.semaphore_signal(barrier, inc=1, device_id={"expert": (c + k) % n}, device_id_type=MESH)
    for k in range(1, nd):
        pl.semaphore_signal(barrier, inc=1, device_id={"dp": (d + k) % nd}, device_id_type=MESH)
    pl.semaphore_signal(barrier, inc=1, device_id={"section": 1 - s}, device_id_type=MESH)

    def remote(src, dst, ss, rsm, **dev):
        return pltpu.make_async_remote_copy(
            src_ref=src, dst_ref=dst, send_sem=ss, recv_sem=rsm, device_id=dev, device_id_type=MESH
        )

    seg_row = segments[...].astype(F32)
    ids = expert_ids[0]
    raw = route_weight[0]
    share = raw / jnp.sum(raw, axis=0, keepdims=True)
    row = lax.broadcasted_iota(jnp.int32, (8, T), 0)
    for g in range(n):
        table = jnp.zeros((8, T), F32)
        for k in range(expert_ids.shape[1]):
            hit = (row < EL) & (row + g * EL == ids[k:k + 1, :])
            table = table + jnp.where(hit, share[k:k + 1, :], 0.0)
        tbl[g] = jnp.where(row == 7, seg_row, table)
    def rt_copy(k):
        to = lax.rem(c + k, n)
        return remote(tbl.at[to], rt.at[c], rtss.at[k - 1], rtrs.at[c], expert=to)

    x = tokens[0].astype(F32)
    scale = lax.rsqrt(jnp.mean(x * x, axis=-1, keepdims=True) + 1e-06)
    nrm[...] = (x * scale * attn_gain[...].astype(F32).reshape(1, W)).astype(BF16)
    lane = lax.broadcasted_iota(jnp.int32, (T, LANES), 1)
    for i in range(3):
        loads[i].wait()
    cosine = cosv[...]
    sine = sinv[...]
    key_cos = jnp.where(lane < 64, cosine, 1.0)
    key_lo = jnp.where(lane < 32, -sine, 0.0)
    key_hi = jnp.where((lane >= 32) & (lane < 64), sine, 0.0)
    pgw[...] = jnp.broadcast_to(page[...].astype(F32), pgw.shape)
    pl.semaphore_wait(barrier, (n - 1) + (nd - 1) + 1)

    steps = win // 2

    def kv_z(k, h):
        at = 2 * k + 2
        return remote(
            kvw.at[2 * k, h], kvw.at[at, h], kvzs.at[k * LKV + h], kvrs.at[(at - 1) * LKV + h],
            expert=lax.rem(c + 2, n),
        )

    def kv_y(k, h):
        to = 2 * k + 1 - 2 * y
        return remote(
            kvw.at[2 * k, h], kvw.at[to, h], kvys.at[k * LKV + h], kvrs.at[(to - 1) * LKV + h],
            expert=ypeer,
        )

    def kv_arrived(j, h):
        remote(
            kvw.at[0, h], kvw.at[j, h], kvzs.at[0], kvrs.at[(j - 1) * LKV + h], expert=ypeer
        ).wait_recv()

    def sends_z(k):
        return (z >= k) & (z + 1 < nz) & (k < steps)

    def sends_y(k):
        if k == 0:
            return y == 0
        return (z >= k) if k < steps else (z >= k) & (y == 1)

    def kv_send(k, h):
        if k < steps:
            @pl.when(sends_z(k))
            def _():
                kv_z(k, h).start()

        @pl.when(sends_y(k))
        def _():
            kv_y(k, h).start()

    for k in range(1, n):
        rt_copy(k).start()
    rt[c] = tbl[c]
    for h2 in range(LKV // 2):
        pair = dot(nrm[...], wkv[:, h2 * 256:(h2 + 1) * 256])
        for o in range(2):
            ch = pair[:, o * LANES:(o + 1) * LANES]
            ch = ch * key_cos + pltpu.roll(ch, 96, 1) * key_lo + pltpu.roll(ch, 32, 1) * key_hi
            kvw[0, 2 * h2 + o] = ch.astype(BF16)
            kv_send(0, 2 * h2 + o)
    for j in range(1, win + 1):
        @pl.when(c < j)
        def _():
            kvw[j] = jnp.zeros(kvw.shape[1:], BF16)

    def dp_copy(k):
        return remote(kvw.at[0], dpr.at[k - 1], dpss.at[k - 1], dprs.at[k - 1], dp=(d + k) % nd)

    def pg_copy(k):
        return remote(pgw, pgr.at[k - 1], pgss.at[k - 1], pgrs.at[k - 1], dp=(d + k) % nd)

    for k in range(1, nd):
        dp_copy(k).start()
        pg_copy(k).start()

    for copy in loads[4:]:
        copy.start()

    loads[3].wait()
    q_cos = cosine * 0.125
    q_lo = jnp.where(lane % 64 < 32, -sine, 0.0) * 0.125
    q_hi = jnp.where(lane % 64 >= 32, sine, 0.0) * 0.125
    for h2 in range(qs.shape[1] // 256):
        pair = dot(nrm[...], wq[:, h2 * 256:(h2 + 1) * 256])
        for o in range(2):
            ch = pair[:, o * LANES:(o + 1) * LANES]
            ch = ch * q_cos + pltpu.roll(ch, 96, 1) * q_lo + pltpu.roll(ch, 32, 1) * q_hi
            at = h2 * 256 + o * LANES
            qs[:, at:at + LANES] = ch.astype(BF16).astype(F32)

    my_rows = pl.ds(pl.multiple_of(s * H, H), H)
    other_rows = pl.ds(pl.multiple_of((1 - s) * H, H), H)
    def rows_of(col, sec):
        return pl.ds(pl.multiple_of((col * 2 + sec) * H, H), H)

    def kv_pass(k, h):
        @pl.when(z >= k)
        def _():
            kv_arrived(2 * k, h)
        kv_send(k, h)

    for k in range(1, steps):
        for h in range(LKV):
            kv_pass(k, h)
    kv_pass(steps, 0)

    def rt_arrived(at):
        remote(tbl.at[0], rt.at[at], rtss.at[0], rtrs.at[at], expert=ypeer).wait_recv()

    for k in range(1, win + 1):
        @pl.when(c >= k)
        def _():
            rt_arrived(c - k)

    eye = lax.broadcasted_iota(jnp.int32, (T, T), 0)
    col = lax.broadcasted_iota(jnp.int32, (T, T), 1)
    seg_col = jnp.sum(jnp.where(eye == col, jnp.broadcast_to(seg_row, (T, T)), 0.0), axis=1, keepdims=True)
    for j in range(win + 1):
        seg_j = rt[jnp.where(c >= j, c - j, c), 7:8, :]
        key_pos = (c - j) * T + col
        allowed = (key_pos >= 0) & (key_pos <= c * T + eye) & (seg_j == seg_col)
        bias[:, j * T:(j + 1) * T] = jnp.where(allowed, 0.0, -1e30)

    heads = []
    keys = (win + 1) * T
    for zh in range(LKV):
        if zh + 1 < LKV:
            kv_pass(steps, zh + 1)
        for k in range(steps):
            @pl.when(c >= 2 * k + 1)
            def _():
                kv_arrived(2 * k + 1, zh)
        kv_head = kvw[:, zh].reshape(keys, LANES)
        group = []
        for m in range(G):
            h = zh * G + m
            ch = qs[:, (h // 2) * LANES:(h // 2 + 1) * LANES]
            if h % 2:
                ch = pltpu.roll(ch, 64, 1)
            group.append(jnp.where(lane < 64, ch, 0.0).astype(BF16))
        q3 = jnp.concatenate(group, axis=0)
        score = lax.dot_general(q3, kv_head, (((1,), (1,)), ((), ())), preferred_element_type=F32)
        score = score.reshape(G, T, keys) + bias[...][None]
        top = jnp.max(score, axis=-1, keepdims=True)
        unscaled = jnp.exp(score - top)
        count = jnp.sum(unscaled, axis=-1, keepdims=True)
        weighted = dot(unscaled.astype(BF16).reshape(G * T, keys), kv_head).reshape(G, T, LANES)
        weighted = weighted / count
        for m in range(G):
            heads.append(weighted[m])
            if len(heads) == 2:
                k = (zh * G + m) // 2
                both = jnp.where(lane < 64, pltpu.roll(heads[0], 64, 1), heads[1])
                attd[:, k * LANES:(k + 1) * LANES] = both.astype(BF16)
                heads = []

    loads[4].wait()
    for k in range(W // 256):
        hp[:, k * 256:(k + 1) * 256] = dot(attd[...], wo[:, k * 256:(k + 1) * 256])
    hps[...] = hp[other_rows, :].astype(BF16)
    head_copy = remote(hps, hpr, hsem.at[0], hsem.at[1], section=1 - s)
    head_copy.start()

    for k in range(1, nd):
        dp_copy(k).wait_recv()
        pg_copy(k).wait_recv()
    target = (d * n + c).astype(F32)
    own_id = pgw[0:1, 0:1]
    for h in range(LKV):
        picked = jnp.where(own_id == target, kvw[0, h].astype(F32), 0.0)
        for k in range(1, nd):
            picked = jnp.where(pgr[k - 1, 0:1, 0:1] == target, dpr[k - 1, h].astype(F32), picked)
        cache[0, :, h * LANES:(h + 1) * LANES] = picked.astype(BF16)

    head_copy.wait_recv()
    resid = tokens[0, my_rows, :].astype(F32) + (hp[my_rows, :] + hpr[...].astype(F32))
    rs[...] = resid
    scale = lax.rsqrt(jnp.mean(resid * resid, axis=-1, keepdims=True) + 1e-06)
    mb[rows_of(c, s), :] = (resid * scale * ffn_gain[...].astype(F32).reshape(1, W)).astype(BF16)

    CH = GATHER_CHUNKS
    HR = H // CH

    def mb_copy(colm, sec, h, ss, **dev):
        rows = pl.ds(pl.multiple_of((colm * 2 + sec) * H + h * HR, HR), HR)
        return remote(mb.at[rows], mb.at[rows], ss, mbrs.at[(colm * 2 + sec) * CH + h], **dev)

    def up_copy(zi, h):
        return mb_copy(zi * 2 + y, s, h, ups.at[zi * CH + h], expert=lax.rem(c + 2, n))

    def down_copy(zi, h):
        return mb_copy(zi * 2 + y, s, h, downs.at[zi * CH + h], expert=lax.rem(c + n - 2, n))

    def y_copy(zi, h):
        return mb_copy(zi * 2 + y, s, h, yss.at[zi * CH + h], expert=ypeer)

    def p_copy(colm, h):
        return mb_copy(colm, s, h, pss.at[colm * CH + h], section=1 - s)

    for h in range(CH):
        @pl.when(z + 1 < nz)
        def _():
            up_copy(z, h).start()

        @pl.when(z >= 1)
        def _():
            down_copy(z, h).start()

        if h < CH // 2:
            y_copy(z, h).start()
        p_copy(c, h).start()
    other_half = pl.ds(pl.multiple_of((1 - s) * HW, HW), HW)
    my_half = pl.ds(pl.multiple_of(s * HW, HW), HW)
    resid_copy = remote(rs.at[:, other_half], rr, rsem_r.at[0], rsem_r.at[1], section=1 - s)
    resid_copy.start()
    for i in range(5, 8):
        loads[i].wait()

    def sec_copy(i, p):
        at = 2 * i + p
        return remote(secs.at[at], secr.at[at], secss.at[at], secrs.at[at], section=1 - s)

    def yr_copy(i, p):
        at = 2 * i + p
        return remote(ysnd.at[at], yrcv.at[at], yrss.at[at], yrrs.at[at], expert=ypeer)

    def zr_copy(zi, p):
        at, to = 2 * zi + p, 2 * z + p
        return remote(zsnd.at[at], zrcv.at[to], zrss.at[at], zrrs.at[to], expert=zi * 2 + y)

    def zr_arrived(zi, p):
        at = 2 * zi + p
        remote(zsnd.at[at], zrcv.at[at], zrss.at[at], zrrs.at[at], expert=zi * 2 + y).wait_recv()

    def near(b):
        return (b == z + 1) | (b == z - 1)

    def near_copy(b, p):
        at = jnp.where(b > z, 0, 2) + p
        return remote(ns.at[at], nr.at[at], nss.at[at], nrs.at[at], expert=b * 2 + y)

    def near_arrived(at):
        remote(ns.at[at], nr.at[at], nss.at[at], nrs.at[at], expert=ypeer).wait_recv()

    def fy_copy(p):
        return remote(fys.at[p], fyr.at[p], fyss.at[p], fyrs.at[p], expert=ypeer)

    to_peer = pl.ds(pl.multiple_of((1 - y) * T, T), T)
    kept = pl.ds(pl.multiple_of(y * T, T), T)

    def layer_of(j):
        k = (j + 1) // 2
        return z + k * (1 - 2 * (j % 2))

    def exists(j):
        return (layer_of(j) >= 0) & (layer_of(j) < nz)

    def pass_on(j):
        zi = layer_of(j)

        @pl.when(exists(j) & (j < 2 * nz - 1))
        def _():
            for h in range(CH):
                mb_copy(zi * 2 + y, s, h, pss.at[0], section=1 - s).wait_recv()

                @pl.when((zi < z) & (z + 1 < nz))
                def _():
                    up_copy(zi, h).start()

                @pl.when((zi > z) & (z >= 1))
                def _():
                    down_copy(zi, h).start()

                y_copy(zi, h).start()
                p_copy(zi * 2 + y, h).start()

    pass_on(1)
    pass_on(2)
    for j in range(3, min(5, 2 * nz - 1)):
        pass_on(j)
    for h in range(CH // 2, CH):
        y_copy(z, h).start()
    for k in range(1, n):
        @pl.when((c < k) | (k > win))
        def _():
            rt_arrived(lax.rem(c + n - k, n))

    def far_return(j, also):
        @pl.when(exists(j) & also)
        def _():
            b = layer_of(j)
            for p in range(2):
                at = 2 * b + p
                yr_copy(b, p).wait_recv()
                zsnd[at] = (sown[at] + yrcv[at].astype(F32)).astype(BF16)
                zr_copy(b, p).start()

    def late_step(j, carry):
        far_return(j, (j + 2 > 2 * nz - 2) | ~exists(j + 2))
        return carry

    def step(turn, carry):
        j = lax.rem(turn + 1, 2 * nz - 1)

        @pl.when(exists(j))
        def _():
            zi = layer_of(j)
            theirs = zi * 2 + (1 - y)
            for h in range(CH):
                mb_copy(theirs, s, h, pss.at[0], section=1 - s).wait_recv()
                p_copy(theirs, h).start()
            for h in range(CH):
                mb_copy(zi * 2 + y, 1 - s, h, pss.at[0], section=1 - s).wait_recv()
            for h in range(CH):
                mb_copy(theirs, 1 - s, h, pss.at[0], section=1 - s).wait_recv()
            rows = pl.ds(pl.multiple_of(zi * (2 * T), 2 * T), 2 * T)
            shares = jnp.concatenate([rt[2 * zi].T, rt[2 * zi + 1].T], axis=0)
            for e in range(EL):
                share_e = shares[:, e:e + 1]
                gate = dot(mb[rows, :], wg[e])
                up = dot(mb[rows, :], wu[e])
                activ = gate / (1.0 + jnp.exp(-gate)) * up
                act[:, e * FL:(e + 1) * FL] = (activ * share_e).astype(BF16)
            for p in range(2):
                cols = pl.ds(pl.multiple_of((1 - s) * HW + p * PW, LANES), PW)
                secs[2 * zi + p] = dot(act[...], wd[:, cols]).astype(BF16)
                sec_copy(zi, p).start()

        @pl.when(exists(j))
        def _():
            b = layer_of(j)
            for p in range(2):
                at = 2 * b + p
                cols = pl.ds(pl.multiple_of(s * HW + p * PW, LANES), PW)
                mine[at] = dot(act[...], wd[:, cols])
                sec_copy(b, p).wait_recv()

                @pl.when(b == z)
                def _():
                    mine[at] = mine[at] + secr[at].astype(F32)

                @pl.when(near(b))
                def _():
                    to = jnp.where(b > z, 0, 2) + p
                    ns[to] = (mine[at] + secr[at].astype(F32)).astype(BF16)
                    near_copy(b, p).start()

                @pl.when((b != z) & ~near(b))
                def _():
                    ysnd[at] = (mine[at, to_peer, :] + secr[at, to_peer, :].astype(F32)).astype(BF16)
                    yr_copy(b, p).start()
                    sown[at] = mine[at, kept, :] + secr[at, kept, :].astype(F32)

        far_return(j - 2, (j >= 5) & exists(j))
        pass_on(turn + 5)
        return carry

    lax.fori_loop(0, 2 * nz - 1, step, 0)

    lax.fori_loop(3, min(5, 2 * nz - 1), late_step, 0)

    for p in range(2):
        for side in range(2):
            @pl.when((z >= 1) if side == 0 else (z + 1 < nz))
            def _():
                near_arrived(2 * side + p)
                mine[2 * z + p] = mine[2 * z + p] + nr[2 * side + p].astype(F32)

        fys[p] = mine[2 * z + p, to_peer, :].astype(BF16)
        fy_copy(p).start()

    lax.fori_loop(5, 2 * nz - 1, late_step, 0)
    resid_copy.wait_recv()
    for p in range(2):
        fy_copy(p).wait_recv()
        sown[2 * z + p] = mine[2 * z + p, kept, :] + fyr[p].astype(F32)

        def far_sum(k, carry):
            zi = lax.rem(z + k, nz)

            @pl.when(~near(zi))
            def _():
                zr_arrived(zi, p)
                sown[2 * z + p] = sown[2 * z + p] + zrcv[2 * zi + p].astype(F32)

            return carry

        lax.fori_loop(1, nz, far_sum, 0)
        cols = slice(p * PW, (p + 1) * PW)
        at = pl.ds(pl.multiple_of(s * HW + p * PW, LANES), PW)
        out[0, my_rows, cols] = (rs[:, at] + sown[2 * z + p, my_rows, :]).astype(BF16)
        out[0, other_rows, cols] = (rr[:, cols] + sown[2 * z + p, other_rows, :]).astype(BF16)

    for p in range(2):
        fy_copy(p).wait_send()
    for k in range(1, n):
        rt_copy(k).wait_send()

    for h in range(LKV):
        for k in range(steps + 1):
            if k < steps:
                @pl.when(sends_z(k))
                def _():
                    kv_z(k, h).wait_send()

            @pl.when(sends_y(k))
            def _():
                kv_y(k, h).wait_send()
    for k in range(1, nd):
        dp_copy(k).wait_send()
        pg_copy(k).wait_send()
    head_copy.wait_send()
    resid_copy.wait_send()
    for zi in range(nz):
        for h in range(CH):
            @pl.when((zi <= z) & (z + 1 < nz))
            def _():
                up_copy(zi, h).wait_send()

            @pl.when((zi >= z) & (z >= 1))
            def _():
                down_copy(zi, h).wait_send()

            y_copy(zi, h).wait_send()
            p_copy(2 * zi, h).wait_send()
            p_copy(2 * zi + 1, h).wait_send()

        for p in range(2):
            @pl.when(near(zi))
            def _():
                near_copy(zi, p).wait_send()

            @pl.when((zi != z) & ~near(zi))
            def _():
                yr_copy(zi, p).wait_send()
                zr_copy(zi, p).wait_send()

        for p in range(2):
            sec_copy(zi, p).wait_send()


def trig(count):
    half = HEAD_WIDTH // 2
    frequency = np.float32(10000.0) ** (
        -(np.arange(half, dtype=np.float32) * np.float32(2.0) / np.float32(HEAD_WIDTH))
    )
    angles = np.arange(count, dtype=np.float32)[:, None] * frequency.astype(np.float32)[None, :]
    reps = LANES // half
    wide = np.tile(angles.astype(np.float64), (1, reps))
    return np.cos(wide).astype(np.float32), np.sin(wide).astype(np.float32)


def shards(
    tokens, segments, attn_gain, query_weight, key_value_weight, out_weight, ffn_gain,
    gate_weight, up_weight, down_weight, expert_ids, route_weight, stream_page_table,
):
    n = lax.axis_size("expert")
    nd = lax.axis_size("dp")
    win = n // 2
    nz = n // 2
    T, W = tokens.shape[1], tokens.shape[2]
    H, HW = T // 2, W // 2
    EL, _, FL = gate_weight.shape
    qw, kw = query_weight.shape[1], key_value_weight.shape[1]
    cosine, sine = trig(T * n)
    down = down_weight.reshape(EL * FL, W)
    vmem = pl.BlockSpec(memory_space=pltpu.VMEM)
    hbm = pl.BlockSpec(memory_space=pl.ANY)
    dma = pltpu.SemaphoreType.DMA
    out, cache = pl.pallas_call(
        functools.partial(layer_kernel, n, nd, win),
        out_shape=(
            jax.ShapeDtypeStruct((1, T, HW), BF16),
            jax.ShapeDtypeStruct((1, T, kw), BF16),
        ),
        in_specs=[vmem] * 7 + [hbm] * 8,
        out_specs=(vmem, vmem),
        scratch_shapes=[
            pltpu.VMEM((W, qw), BF16),
            pltpu.VMEM((W, kw), BF16),
            pltpu.VMEM((qw, W), BF16),
            pltpu.VMEM((EL, W, FL), BF16),
            pltpu.VMEM((EL, W, FL), BF16),
            pltpu.VMEM((EL * FL, W), BF16),
            pltpu.VMEM((T, LANES), F32),
            pltpu.VMEM((T, LANES), F32),
            pltpu.VMEM((n, 8, T), F32),
            pltpu.VMEM((n, 8, T), F32),
            pltpu.VMEM((T, W), BF16),
            pltpu.VMEM((win + 1, kw // LANES, T, LANES), BF16),
            pltpu.VMEM((nd - 1, kw // LANES, T, LANES), BF16),
            pltpu.VMEM((8, LANES), F32),
            pltpu.VMEM((nd - 1, 8, LANES), F32),
            pltpu.VMEM((T, qw), F32),
            pltpu.VMEM((T, (win + 1) * T), F32),
            pltpu.VMEM((T, qw), BF16),
            pltpu.VMEM((T, W), F32),
            pltpu.VMEM((H, W), BF16),
            pltpu.VMEM((H, W), BF16),
            pltpu.VMEM((H, W), F32),
            pltpu.VMEM((H, HW), F32),
            pltpu.VMEM((n * T, W), BF16),
            pltpu.VMEM((2 * T, EL * FL), BF16),
            pltpu.VMEM((2 * nz, 2 * T, HW // 2), BF16),
            pltpu.VMEM((2 * nz, 2 * T, HW // 2), BF16),
            pltpu.VMEM((2 * nz, 2 * T, HW // 2), F32),
            pltpu.VMEM((2 * nz, T, HW // 2), BF16),
            pltpu.VMEM((2 * nz, T, HW // 2), BF16),
            pltpu.VMEM((2 * nz, T, HW // 2), F32),
            pltpu.VMEM((2 * nz, T, HW // 2), BF16),
            pltpu.VMEM((2 * nz, T, HW // 2), BF16),
            pltpu.VMEM((4, 2 * T, HW // 2), BF16),
            pltpu.VMEM((4, 2 * T, HW // 2), BF16),
            pltpu.VMEM((2, T, HW // 2), BF16),
            pltpu.VMEM((2, T, HW // 2), BF16),
            dma((8,)),
            dma((win // 2 * (kw // LANES),)), dma(((win // 2 + 1) * (kw // LANES),)), dma((win * (kw // LANES),)),
            dma((nd - 1,)), dma((nd - 1,)), dma((nd - 1,)), dma((nd - 1,)),
            dma((2,)), dma((2,)),
            dma((nz * GATHER_CHUNKS,)), dma((nz * GATHER_CHUNKS,)), dma((nz * GATHER_CHUNKS,)),
            dma((n * GATHER_CHUNKS,)), dma((2 * n * GATHER_CHUNKS,)),
            dma((n,)), dma((n,)), dma((n,)), dma((n,)), dma((n,)), dma((n,)),
            dma((4,)), dma((4,)), dma((2,)), dma((2,)), dma((n,)), dma((n,)),
        ],
        compiler_params=pltpu.CompilerParams(
            collective_id=0, has_side_effects=True, vmem_limit_bytes=58 * 1024 * 1024
        ),
    )(
        tokens, segments, attn_gain, ffn_gain, expert_ids.transpose(0, 2, 1),
        route_weight.transpose(0, 2, 1), stream_page_table, jnp.asarray(cosine), jnp.asarray(sine),
        query_weight, key_value_weight, out_weight, gate_weight, up_weight, down,
    )

    def hand_over(out_in, cache_in, out_to, cache_to):
        out_to[...] = out_in[...]
        cache_to[...] = cache_in[...]

    return pl.pallas_call(
        hand_over,
        out_shape=(jax.ShapeDtypeStruct(out.shape, BF16), jax.ShapeDtypeStruct(cache.shape, BF16)),
        in_specs=[vmem, vmem],
        out_specs=(vmem, vmem),
    )(out, cache)


def solution(mesh):
    in_specs = (
        P("dp", "expert", None),
        P("dp", "expert"),
        P(),
        P(None, "section"),
        P(None, "section"),
        P("section", None),
        P(),
        P("expert", None, "section"),
        P("expert", None, "section"),
        P("expert", "section", None),
        P("dp", "expert", None),
        P("dp", "expert", None),
        P("dp", "expert"),
    )
    out_specs = (P("dp", "expert", "section"), P(("dp", "expert"), None, "section"))
    return jax.shard_map(shards, mesh=mesh, in_specs=in_specs, out_specs=out_specs, check_vma=False)
```

```python
import functools
import math

import jax
import jax.numpy as jnp
import numpy as np
from jax import lax
from jax.experimental import pallas as pl
from jax.experimental.pallas import tpu as pltpu
from jax.sharding import PartitionSpec as P

QUERY_HEADS = 24
KEYVALUE_HEADS = 8
HEAD_WIDTH = 64
LANES = 128
GATHER_CHUNKS = 2
MESH = pl.DeviceIdType.MESH
F32 = jnp.float32
BF16 = jnp.bfloat16


def dot(a, b):
    return jnp.dot(a, b, preferred_element_type=F32)


def layer_kernel(
    n, nd, win,
    tokens, segments, attn_gain, ffn_gain, expert_ids, route_weight, page,
    cos_hbm, sin_hbm, wq_hbm, wkv_hbm, wo_hbm, wg_hbm, wu_hbm, wd_hbm,
    out, cache,
    wq, wkv, wo, wg, wu, wd, cosv, sinv,
    tbl, rt, nrm, kvw, dpr, pgw, pgr, qs, bias, attd, hp, hps, hpr, rs, rr, mb,
    act, secs, secr, mine, ysnd, yrcv, sown, zsnd, zrcv, ns, nr, fys, fyr,
    wsem, kvzs, kvys, kvrs, dpss, dprs, pgss, pgrs, hsem, rsem_r, ups, downs, yss, pss, mbrs,
    secss, secrs, yrss, yrrs, zrss, zrrs, nss, nrs, fyss, fyrs, rtss, rtrs,
):
    s = lax.axis_index("section")
    d = lax.axis_index("dp")
    c = lax.axis_index("expert")
    nz = n // 2
    z = c // 2
    y = c % 2
    T = tokens.shape[1]
    H = T // 2
    W = tokens.shape[2]
    HW = W // 2
    PW = HW // 2
    EL = wg.shape[0]
    FL = wg.shape[2]
    LKV = wkv.shape[1] // LANES
    G = QUERY_HEADS // KEYVALUE_HEADS
    ypeer = z * 2 + (1 - y)

    def local(src, dst, i):
        return pltpu.make_async_copy(src, dst, wsem.at[i])

    loads = [
        local(wkv_hbm, wkv, 0),
        local(cos_hbm.at[pl.ds(pl.multiple_of(c * T, T), T)], cosv, 1),
        local(sin_hbm.at[pl.ds(pl.multiple_of(c * T, T), T)], sinv, 2),
        local(wq_hbm, wq, 3),
        local(wo_hbm, wo, 4),
        local(wg_hbm, wg, 5),
        local(wu_hbm, wu, 6),
        local(wd_hbm, wd, 7),
    ]
    for copy in loads[:4]:
        copy.start()

    barrier = pltpu.get_barrier_semaphore()
    for k in range(1, n):
        pl.semaphore_signal(barrier, inc=1, device_id={"expert": (c + k) % n}, device_id_type=MESH)
    for k in range(1, nd):
        pl.semaphore_signal(barrier, inc=1, device_id={"dp": (d + k) % nd}, device_id_type=MESH)
    pl.semaphore_signal(barrier, inc=1, device_id={"section": 1 - s}, device_id_type=MESH)

    def remote(src, dst, ss, rsm, **dev):
        return pltpu.make_async_remote_copy(
            src_ref=src, dst_ref=dst, send_sem=ss, recv_sem=rsm, device_id=dev, device_id_type=MESH
        )

    seg_row = segments[...].astype(F32)
    ids = expert_ids[0]
    raw = route_weight[0]
    share = raw / jnp.sum(raw, axis=0, keepdims=True)
    row = lax.broadcasted_iota(jnp.int32, (8, T), 0)
    for g in range(n):
        table = jnp.zeros((8, T), F32)
        for k in range(expert_ids.shape[1]):
            hit = (row < EL) & (row + g * EL == ids[k:k + 1, :])
            table = table + jnp.where(hit, share[k:k + 1, :], 0.0)
        tbl[g] = jnp.where(row == 7, seg_row, table)
    def rt_copy(k):
        to = lax.rem(c + k, n)
        return remote(tbl.at[to], rt.at[c], rtss.at[k - 1], rtrs.at[c], expert=to)

    x = tokens[0].astype(F32)
    scale = lax.rsqrt(jnp.mean(x * x, axis=-1, keepdims=True) + 1e-06)
    nrm[...] = (x * scale * attn_gain[...].astype(F32).reshape(1, W)).astype(BF16)
    lane = lax.broadcasted_iota(jnp.int32, (T, LANES), 1)
    for i in range(3):
        loads[i].wait()
    cosine = cosv[...]
    sine = sinv[...]
    key_cos = jnp.where(lane < 64, cosine, 1.0)
    key_lo = jnp.where(lane < 32, -sine, 0.0)
    key_hi = jnp.where((lane >= 32) & (lane < 64), sine, 0.0)
    pgw[...] = jnp.broadcast_to(page[...].astype(F32), pgw.shape)
    for h2 in range(LKV // 2):
        pair = dot(nrm[...], wkv[:, h2 * 256:(h2 + 1) * 256])
        for o in range(2):
            ch = pair[:, o * LANES:(o + 1) * LANES]
            ch = ch * key_cos + pltpu.roll(ch, 96, 1) * key_lo + pltpu.roll(ch, 32, 1) * key_hi
            kvw[0, 2 * h2 + o] = ch.astype(BF16)
    for j in range(1, win + 1):
        @pl.when(c < j)
        def _():
            kvw[j] = jnp.zeros(kvw.shape[1:], BF16)

    def dp_copy(k):
        return remote(kvw.at[0], dpr.at[k - 1], dpss.at[k - 1], dprs.at[k - 1], dp=(d + k) % nd)

    pl.semaphore_wait(barrier, (n - 1) + (nd - 1) + 1)

    steps = win // 2

    def kv_z(k, h):
        at = 2 * k + 2
        return remote(
            kvw.at[2 * k, h], kvw.at[at, h], kvzs.at[k * LKV + h], kvrs.at[(at - 1) * LKV + h],
            expert=lax.rem(c + 2, n),
        )

    def kv_y(k, h):
        to = 2 * k + 1 - 2 * y
        return remote(
            kvw.at[2 * k, h], kvw.at[to, h], kvys.at[k * LKV + h], kvrs.at[(to - 1) * LKV + h],
            expert=ypeer,
        )

    def kv_arrived(j, h):
        remote(
            kvw.at[0, h], kvw.at[j, h], kvzs.at[0], kvrs.at[(j - 1) * LKV + h], expert=ypeer
        ).wait_recv()

    def sends_z(k):
        return (z >= k) & (z + 1 < nz) & (k < steps)

    def sends_y(k):
        if k == 0:
            return y == 0
        return (z >= k) if k < steps else (z >= k) & (y == 1)

    def kv_send(k, h):
        if k < steps:
            @pl.when(sends_z(k))
            def _():
                kv_z(k, h).start()

        @pl.when(sends_y(k))
        def _():
            kv_y(k, h).start()

    for h in range(LKV):
        kv_send(0, h)

    for k in range(1, n):
        rt_copy(k).start()
    rt[c] = tbl[c]

    def pg_copy(k):
        return remote(pgw, pgr.at[k - 1], pgss.at[k - 1], pgrs.at[k - 1], dp=(d + k) % nd)

    for k in range(1, nd):
        dp_copy(k).start()
        pg_copy(k).start()

    for copy in loads[4:]:
        copy.start()

    loads[3].wait()
    q_cos = cosine * 0.125
    q_lo = jnp.where(lane % 64 < 32, -sine, 0.0) * 0.125
    q_hi = jnp.where(lane % 64 >= 32, sine, 0.0) * 0.125
    for h2 in range(qs.shape[1] // 256):
        pair = dot(nrm[...], wq[:, h2 * 256:(h2 + 1) * 256])
        for o in range(2):
            ch = pair[:, o * LANES:(o + 1) * LANES]
            ch = ch * q_cos + pltpu.roll(ch, 96, 1) * q_lo + pltpu.roll(ch, 32, 1) * q_hi
            at = h2 * 256 + o * LANES
            qs[:, at:at + LANES] = ch.astype(BF16).astype(F32)

    my_rows = pl.ds(pl.multiple_of(s * H, H), H)
    other_rows = pl.ds(pl.multiple_of((1 - s) * H, H), H)
    def rows_of(col, sec):
        return pl.ds(pl.multiple_of((col * 2 + sec) * H, H), H)

    def kv_pass(k, h):
        @pl.when(z >= k)
        def _():
            kv_arrived(2 * k, h)
        kv_send(k, h)

    for k in range(1, steps):
        for h in range(LKV):
            kv_pass(k, h)
    kv_pass(steps, 0)

    def rt_arrived(at):
        remote(tbl.at[0], rt.at[at], rtss.at[0], rtrs.at[at], expert=ypeer).wait_recv()

    for k in range(1, win + 1):
        @pl.when(c >= k)
        def _():
            rt_arrived(c - k)

    eye = lax.broadcasted_iota(jnp.int32, (T, T), 0)
    col = lax.broadcasted_iota(jnp.int32, (T, T), 1)
    seg_col = jnp.sum(jnp.where(eye == col, jnp.broadcast_to(seg_row, (T, T)), 0.0), axis=1, keepdims=True)
    for j in range(win + 1):
        seg_j = rt[jnp.where(c >= j, c - j, c), 7:8, :]
        key_pos = (c - j) * T + col
        allowed = (key_pos >= 0) & (key_pos <= c * T + eye) & (seg_j == seg_col)
        bias[:, j * T:(j + 1) * T] = jnp.where(allowed, 0.0, -1e30)

    heads = []
    keys = (win + 1) * T
    for zh in range(LKV):
        if zh + 1 < LKV:
            kv_pass(steps, zh + 1)
        for k in range(steps):
            @pl.when(c >= 2 * k + 1)
            def _():
                kv_arrived(2 * k + 1, zh)
        kv_head = kvw[:, zh].reshape(keys, LANES)
        group = []
        for m in range(G):
            h = zh * G + m
            ch = qs[:, (h // 2) * LANES:(h // 2 + 1) * LANES]
            if h % 2:
                ch = pltpu.roll(ch, 64, 1)
            group.append(jnp.where(lane < 64, ch, 0.0).astype(BF16))
        q3 = jnp.concatenate(group, axis=0)
        score = lax.dot_general(q3, kv_head, (((1,), (1,)), ((), ())), preferred_element_type=F32)
        score = score.reshape(G, T, keys) + bias[...][None]
        top = jnp.max(score, axis=-1, keepdims=True)
        unscaled = jnp.exp(score - top)
        count = jnp.sum(unscaled, axis=-1, keepdims=True)
        weighted = dot(unscaled.astype(BF16).reshape(G * T, keys), kv_head).reshape(G, T, LANES)
        weighted = weighted / count
        for m in range(G):
            heads.append(weighted[m])
            if len(heads) == 2:
                k = (zh * G + m) // 2
                both = jnp.where(lane < 64, pltpu.roll(heads[0], 64, 1), heads[1])
                attd[:, k * LANES:(k + 1) * LANES] = both.astype(BF16)
                heads = []

    loads[4].wait()
    for k in range(W // 256):
        hp[:, k * 256:(k + 1) * 256] = dot(attd[...], wo[:, k * 256:(k + 1) * 256])
    hps[...] = hp[other_rows, :].astype(BF16)
    head_copy = remote(hps, hpr, hsem.at[0], hsem.at[1], section=1 - s)
    head_copy.start()

    for k in range(1, nd):
        dp_copy(k).wait_recv()
        pg_copy(k).wait_recv()
    target = (d * n + c).astype(F32)
    own_id = pgw[0:1, 0:1]
    for h in range(LKV):
        picked = jnp.where(own_id == target, kvw[0, h].astype(F32), 0.0)
        for k in range(1, nd):
            picked = jnp.where(pgr[k - 1, 0:1, 0:1] == target, dpr[k - 1, h].astype(F32), picked)
        cache[0, :, h * LANES:(h + 1) * LANES] = picked.astype(BF16)

    head_copy.wait_recv()
    resid = tokens[0, my_rows, :].astype(F32) + (hp[my_rows, :] + hpr[...].astype(F32))
    rs[...] = resid
    scale = lax.rsqrt(jnp.mean(resid * resid, axis=-1, keepdims=True) + 1e-06)
    mb[rows_of(c, s), :] = (resid * scale * ffn_gain[...].astype(F32).reshape(1, W)).astype(BF16)

    CH = GATHER_CHUNKS
    HR = H // CH

    def mb_copy(colm, sec, h, ss, **dev):
        rows = pl.ds(pl.multiple_of((colm * 2 + sec) * H + h * HR, HR), HR)
        return remote(mb.at[rows], mb.at[rows], ss, mbrs.at[(colm * 2 + sec) * CH + h], **dev)

    def up_copy(zi, h):
        return mb_copy(zi * 2 + y, s, h, ups.at[zi * CH + h], expert=lax.rem(c + 2, n))

    def down_copy(zi, h):
        return mb_copy(zi * 2 + y, s, h, downs.at[zi * CH + h], expert=lax.rem(c + n - 2, n))

    def y_copy(zi, h):
        return mb_copy(zi * 2 + y, s, h, yss.at[zi * CH + h], expert=ypeer)

    def p_copy(colm, h):
        return mb_copy(colm, s, h, pss.at[colm * CH + h], section=1 - s)

    for h in range(CH):
        @pl.when(z + 1 < nz)
        def _():
            up_copy(z, h).start()

        @pl.when(z >= 1)
        def _():
            down_copy(z, h).start()

        if h < CH // 2:
            y_copy(z, h).start()
        p_copy(c, h).start()
    other_half = pl.ds(pl.multiple_of((1 - s) * HW, HW), HW)
    my_half = pl.ds(pl.multiple_of(s * HW, HW), HW)
    resid_copy = remote(rs.at[:, other_half], rr, rsem_r.at[0], rsem_r.at[1], section=1 - s)
    resid_copy.start()
    for i in range(5, 8):
        loads[i].wait()

    def sec_copy(i, p):
        at = 2 * i + p
        return remote(secs.at[at], secr.at[at], secss.at[at], secrs.at[at], section=1 - s)

    def yr_copy(i, p):
        at = 2 * i + p
        return remote(ysnd.at[at], yrcv.at[at], yrss.at[at], yrrs.at[at], expert=ypeer)

    def zr_copy(zi, p):
        at, to = 2 * zi + p, 2 * z + p
        return remote(zsnd.at[at], zrcv.at[to], zrss.at[at], zrrs.at[to], expert=zi * 2 + y)

    def zr_arrived(zi, p):
        at = 2 * zi + p
        remote(zsnd.at[at], zrcv.at[at], zrss.at[at], zrrs.at[at], expert=zi * 2 + y).wait_recv()

    def near(b):
        return (b == z + 1) | (b == z - 1)

    def near_copy(b, p):
        at = jnp.where(b > z, 0, 2) + p
        return remote(ns.at[at], nr.at[at], nss.at[at], nrs.at[at], expert=b * 2 + y)

    def near_arrived(at):
        remote(ns.at[at], nr.at[at], nss.at[at], nrs.at[at], expert=ypeer).wait_recv()

    def fy_copy(p):
        return remote(fys.at[p], fyr.at[p], fyss.at[p], fyrs.at[p], expert=ypeer)

    to_peer = pl.ds(pl.multiple_of((1 - y) * T, T), T)
    kept = pl.ds(pl.multiple_of(y * T, T), T)

    def layer_of(j):
        k = (j + 1) // 2
        return z + k * (1 - 2 * (j % 2))

    def exists(j):
        return (layer_of(j) >= 0) & (layer_of(j) < nz)

    def pass_on(j):
        zi = layer_of(j)

        @pl.when(exists(j) & (j < 2 * nz - 1))
        def _():
            for h in range(CH):
                mb_copy(zi * 2 + y, s, h, pss.at[0], section=1 - s).wait_recv()

                @pl.when((zi < z) & (z + 1 < nz))
                def _():
                    up_copy(zi, h).start()

                @pl.when((zi > z) & (z >= 1))
                def _():
                    down_copy(zi, h).start()

                y_copy(zi, h).start()
                p_copy(zi * 2 + y, h).start()

    pass_on(1)
    pass_on(2)
    for j in range(3, min(5, 2 * nz - 1)):
        pass_on(j)
    for h in range(CH // 2, CH):
        y_copy(z, h).start()
    for k in range(1, n):
        @pl.when((c < k) | (k > win))
        def _():
            rt_arrived(lax.rem(c + n - k, n))

    def far_return(j, also):
        @pl.when(exists(j) & also)
        def _():
            b = layer_of(j)
            for p in range(2):
                at = 2 * b + p
                yr_copy(b, p).wait_recv()
                zsnd[at] = (sown[at] + yrcv[at].astype(F32)).astype(BF16)
                zr_copy(b, p).start()

    def late_step(j, carry):
        far_return(j, (j + 2 > 2 * nz - 2) | ~exists(j + 2))
        return carry

    def step(turn, carry):
        j = lax.rem(turn + 1, 2 * nz - 1)

        @pl.when(exists(j))
        def _():
            zi = layer_of(j)
            theirs = zi * 2 + (1 - y)
            for h in range(CH):
                mb_copy(theirs, s, h, pss.at[0], section=1 - s).wait_recv()
                p_copy(theirs, h).start()
            for h in range(CH):
                mb_copy(zi * 2 + y, 1 - s, h, pss.at[0], section=1 - s).wait_recv()
            for h in range(CH):
                mb_copy(theirs, 1 - s, h, pss.at[0], section=1 - s).wait_recv()
            rows = pl.ds(pl.multiple_of(zi * (2 * T), 2 * T), 2 * T)
            shares = jnp.concatenate([rt[2 * zi].T, rt[2 * zi + 1].T], axis=0)
            for e in range(EL):
                share_e = shares[:, e:e + 1]
                gate = dot(mb[rows, :], wg[e])
                up = dot(mb[rows, :], wu[e])
                activ = gate / (1.0 + jnp.exp(-gate)) * up
                act[:, e * FL:(e + 1) * FL] = (activ * share_e).astype(BF16)
            for p in range(2):
                cols = pl.ds(pl.multiple_of((1 - s) * HW + p * PW, LANES), PW)
                secs[2 * zi + p] = dot(act[...], wd[:, cols]).astype(BF16)
                sec_copy(zi, p).start()

        pass_on(turn + 5)

        @pl.when(exists(j))
        def _():
            b = layer_of(j)
            for p in range(2):
                at = 2 * b + p
                cols = pl.ds(pl.multiple_of(s * HW + p * PW, LANES), PW)
                mine[at] = dot(act[...], wd[:, cols])
                sec_copy(b, p).wait_recv()

                @pl.when(b == z)
                def _():
                    mine[at] = mine[at] + secr[at].astype(F32)

                @pl.when(near(b))
                def _():
                    to = jnp.where(b > z, 0, 2) + p
                    ns[to] = (mine[at] + secr[at].astype(F32)).astype(BF16)
                    near_copy(b, p).start()

                @pl.when((b != z) & ~near(b))
                def _():
                    ysnd[at] = (mine[at, to_peer, :] + secr[at, to_peer, :].astype(F32)).astype(BF16)
                    yr_copy(b, p).start()
                    sown[at] = mine[at, kept, :] + secr[at, kept, :].astype(F32)

        far_return(j - 2, (j >= 5) & exists(j))
        return carry

    lax.fori_loop(0, 2 * nz - 1, step, 0)

    lax.fori_loop(3, min(5, 2 * nz - 1), late_step, 0)

    for p in range(2):
        for side in range(2):
            @pl.when((z >= 1) if side == 0 else (z + 1 < nz))
            def _():
                near_arrived(2 * side + p)
                mine[2 * z + p] = mine[2 * z + p] + nr[2 * side + p].astype(F32)

        fys[p] = mine[2 * z + p, to_peer, :].astype(BF16)
        fy_copy(p).start()

    lax.fori_loop(5, 2 * nz - 1, late_step, 0)
    resid_copy.wait_recv()
    for p in range(2):
        fy_copy(p).wait_recv()
        sown[2 * z + p] = mine[2 * z + p, kept, :] + fyr[p].astype(F32)

        def far_sum(k, carry):
            zi = lax.rem(z + k, nz)

            @pl.when(~near(zi))
            def _():
                zr_arrived(zi, p)
                sown[2 * z + p] = sown[2 * z + p] + zrcv[2 * zi + p].astype(F32)

            return carry

        lax.fori_loop(1, nz, far_sum, 0)
        cols = slice(p * PW, (p + 1) * PW)
        at = pl.ds(pl.multiple_of(s * HW + p * PW, LANES), PW)
        out[0, my_rows, cols] = (rs[:, at] + sown[2 * z + p, my_rows, :]).astype(BF16)
        out[0, other_rows, cols] = (rr[:, cols] + sown[2 * z + p, other_rows, :]).astype(BF16)

    for p in range(2):
        fy_copy(p).wait_send()
    for k in range(1, n):
        rt_copy(k).wait_send()

    for h in range(LKV):
        for k in range(steps + 1):
            if k < steps:
                @pl.when(sends_z(k))
                def _():
                    kv_z(k, h).wait_send()

            @pl.when(sends_y(k))
            def _():
                kv_y(k, h).wait_send()
    for k in range(1, nd):
        dp_copy(k).wait_send()
        pg_copy(k).wait_send()
    head_copy.wait_send()
    resid_copy.wait_send()
    for zi in range(nz):
        for h in range(CH):
            @pl.when((zi <= z) & (z + 1 < nz))
            def _():
                up_copy(zi, h).wait_send()

            @pl.when((zi >= z) & (z >= 1))
            def _():
                down_copy(zi, h).wait_send()

            y_copy(zi, h).wait_send()
            p_copy(2 * zi, h).wait_send()
            p_copy(2 * zi + 1, h).wait_send()

        for p in range(2):
            @pl.when(near(zi))
            def _():
                near_copy(zi, p).wait_send()

            @pl.when((zi != z) & ~near(zi))
            def _():
                yr_copy(zi, p).wait_send()
                zr_copy(zi, p).wait_send()

        for p in range(2):
            sec_copy(zi, p).wait_send()


def trig(count):
    half = HEAD_WIDTH // 2
    frequency = np.float32(10000.0) ** (
        -(np.arange(half, dtype=np.float32) * np.float32(2.0) / np.float32(HEAD_WIDTH))
    )
    angles = np.arange(count, dtype=np.float32)[:, None] * frequency.astype(np.float32)[None, :]
    reps = LANES // half
    wide = np.tile(angles.astype(np.float64), (1, reps))
    return np.cos(wide).astype(np.float32), np.sin(wide).astype(np.float32)


def shards(
    tokens, segments, attn_gain, query_weight, key_value_weight, out_weight, ffn_gain,
    gate_weight, up_weight, down_weight, expert_ids, route_weight, stream_page_table,
):
    n = lax.axis_size("expert")
    nd = lax.axis_size("dp")
    win = n // 2
    nz = n // 2
    T, W = tokens.shape[1], tokens.shape[2]
    H, HW = T // 2, W // 2
    EL, _, FL = gate_weight.shape
    qw, kw = query_weight.shape[1], key_value_weight.shape[1]
    cosine, sine = trig(T * n)
    down = down_weight.reshape(EL * FL, W)
    vmem = pl.BlockSpec(memory_space=pltpu.VMEM)
    hbm = pl.BlockSpec(memory_space=pl.ANY)
    dma = pltpu.SemaphoreType.DMA
    out, cache = pl.pallas_call(
        functools.partial(layer_kernel, n, nd, win),
        out_shape=(
            jax.ShapeDtypeStruct((1, T, HW), BF16),
            jax.ShapeDtypeStruct((1, T, kw), BF16),
        ),
        in_specs=[vmem] * 7 + [hbm] * 8,
        out_specs=(vmem, vmem),
        scratch_shapes=[
            pltpu.VMEM((W, qw), BF16),
            pltpu.VMEM((W, kw), BF16),
            pltpu.VMEM((qw, W), BF16),
            pltpu.VMEM((EL, W, FL), BF16),
            pltpu.VMEM((EL, W, FL), BF16),
            pltpu.VMEM((EL * FL, W), BF16),
            pltpu.VMEM((T, LANES), F32),
            pltpu.VMEM((T, LANES), F32),
            pltpu.VMEM((n, 8, T), F32),
            pltpu.VMEM((n, 8, T), F32),
            pltpu.VMEM((T, W), BF16),
            pltpu.VMEM((win + 1, kw // LANES, T, LANES), BF16),
            pltpu.VMEM((nd - 1, kw // LANES, T, LANES), BF16),
            pltpu.VMEM((8, LANES), F32),
            pltpu.VMEM((nd - 1, 8, LANES), F32),
            pltpu.VMEM((T, qw), F32),
            pltpu.VMEM((T, (win + 1) * T), F32),
            pltpu.VMEM((T, qw), BF16),
            pltpu.VMEM((T, W), F32),
            pltpu.VMEM((H, W), BF16),
            pltpu.VMEM((H, W), BF16),
            pltpu.VMEM((H, W), F32),
            pltpu.VMEM((H, HW), F32),
            pltpu.VMEM((n * T, W), BF16),
            pltpu.VMEM((2 * T, EL * FL), BF16),
            pltpu.VMEM((2 * nz, 2 * T, HW // 2), BF16),
            pltpu.VMEM((2 * nz, 2 * T, HW // 2), BF16),
            pltpu.VMEM((2 * nz, 2 * T, HW // 2), F32),
            pltpu.VMEM((2 * nz, T, HW // 2), BF16),
            pltpu.VMEM((2 * nz, T, HW // 2), BF16),
            pltpu.VMEM((2 * nz, T, HW // 2), F32),
            pltpu.VMEM((2 * nz, T, HW // 2), BF16),
            pltpu.VMEM((2 * nz, T, HW // 2), BF16),
            pltpu.VMEM((4, 2 * T, HW // 2), BF16),
            pltpu.VMEM((4, 2 * T, HW // 2), BF16),
            pltpu.VMEM((2, T, HW // 2), BF16),
            pltpu.VMEM((2, T, HW // 2), BF16),
            dma((8,)),
            dma((win // 2 * (kw // LANES),)), dma(((win // 2 + 1) * (kw // LANES),)), dma((win * (kw // LANES),)),
            dma((nd - 1,)), dma((nd - 1,)), dma((nd - 1,)), dma((nd - 1,)),
            dma((2,)), dma((2,)),
            dma((nz * GATHER_CHUNKS,)), dma((nz * GATHER_CHUNKS,)), dma((nz * GATHER_CHUNKS,)),
            dma((n * GATHER_CHUNKS,)), dma((2 * n * GATHER_CHUNKS,)),
            dma((n,)), dma((n,)), dma((n,)), dma((n,)), dma((n,)), dma((n,)),
            dma((4,)), dma((4,)), dma((2,)), dma((2,)), dma((n,)), dma((n,)),
        ],
        compiler_params=pltpu.CompilerParams(
            collective_id=0, has_side_effects=True, vmem_limit_bytes=58 * 1024 * 1024
        ),
    )(
        tokens, segments, attn_gain, ffn_gain, expert_ids.transpose(0, 2, 1),
        route_weight.transpose(0, 2, 1), stream_page_table, jnp.asarray(cosine), jnp.asarray(sine),
        query_weight, key_value_weight, out_weight, gate_weight, up_weight, down,
    )

    def hand_over(out_in, cache_in, out_to, cache_to):
        out_to[...] = out_in[...]
        cache_to[...] = cache_in[...]

    return pl.pallas_call(
        hand_over,
        out_shape=(jax.ShapeDtypeStruct(out.shape, BF16), jax.ShapeDtypeStruct(cache.shape, BF16)),
        in_specs=[vmem, vmem],
        out_specs=(vmem, vmem),
    )(out, cache)


def solution(mesh):
    in_specs = (
        P("dp", "expert", None),
        P("dp", "expert"),
        P(),
        P(None, "section"),
        P(None, "section"),
        P("section", None),
        P(),
        P("expert", None, "section"),
        P("expert", None, "section"),
        P("expert", "section", None),
        P("dp", "expert", None),
        P("dp", "expert", None),
        P("dp", "expert"),
    )
    out_specs = (P("dp", "expert", "section"), P(("dp", "expert"), None, "section"))
    return jax.shard_map(shards, mesh=mesh, in_specs=in_specs, out_specs=out_specs, check_vma=False)
```

```python
import functools
import math

import jax
import jax.numpy as jnp
import numpy as np
from jax import lax
from jax.experimental import pallas as pl
from jax.experimental.pallas import tpu as pltpu
from jax.sharding import PartitionSpec as P

QUERY_HEADS = 24
KEYVALUE_HEADS = 8
HEAD_WIDTH = 64
LANES = 128
GATHER_CHUNKS = 2
MESH = pl.DeviceIdType.MESH
F32 = jnp.float32
BF16 = jnp.bfloat16


def dot(a, b):
    return jnp.dot(a, b, preferred_element_type=F32)


def layer_kernel(
    n, nd, win,
    tokens, segments, attn_gain, ffn_gain, expert_ids, route_weight, page,
    cos_hbm, sin_hbm, wq_hbm, wkv_hbm, wo_hbm, wg_hbm, wu_hbm, wd_hbm,
    out, cache,
    wq, wkv, wo, wg, wu, wd, cosv, sinv,
    tbl, rt, nrm, kvw, dpr, pgw, pgr, qs, bias, attd, hp, hps, hpr, rs, rr, mb,
    act, secs, secr, mine, ysnd, yrcv, sown, zsnd, zrcv, ns, nr, fys, fyr,
    wsem, kvzs, kvys, kvrs, dpss, dprs, pgss, pgrs, hsem, rsem_r, ups, downs, yss, pss, mbrs,
    secss, secrs, yrss, yrrs, zrss, zrrs, nss, nrs, fyss, fyrs, rtss, rtrs,
):
    s = lax.axis_index("section")
    d = lax.axis_index("dp")
    c = lax.axis_index("expert")
    nz = n // 2
    z = c // 2
    y = c % 2
    T = tokens.shape[1]
    H = T // 2
    W = tokens.shape[2]
    HW = W // 2
    PW = HW // 2
    EL = wg.shape[0]
    FL = wg.shape[2]
    LKV = wkv.shape[1] // LANES
    G = QUERY_HEADS // KEYVALUE_HEADS
    ypeer = z * 2 + (1 - y)

    def local(src, dst, i):
        return pltpu.make_async_copy(src, dst, wsem.at[i])

    loads = [
        local(wkv_hbm, wkv, 0),
        local(cos_hbm.at[pl.ds(pl.multiple_of(c * T, T), T)], cosv, 1),
        local(sin_hbm.at[pl.ds(pl.multiple_of(c * T, T), T)], sinv, 2),
        local(wq_hbm, wq, 3),
        local(wo_hbm, wo, 4),
        local(wg_hbm, wg, 5),
        local(wu_hbm, wu, 6),
        local(wd_hbm, wd, 7),
    ]
    for copy in loads[:4]:
        copy.start()

    barrier = pltpu.get_barrier_semaphore()
    for k in range(1, n):
        pl.semaphore_signal(barrier, inc=1, device_id={"expert": (c + k) % n}, device_id_type=MESH)
    for k in range(1, nd):
        pl.semaphore_signal(barrier, inc=1, device_id={"dp": (d + k) % nd}, device_id_type=MESH)
    pl.semaphore_signal(barrier, inc=1, device_id={"section": 1 - s}, device_id_type=MESH)

    def remote(src, dst, ss, rsm, **dev):
        return pltpu.make_async_remote_copy(
            src_ref=src, dst_ref=dst, send_sem=ss, recv_sem=rsm, device_id=dev, device_id_type=MESH
        )

    seg_row = segments[...].astype(F32)
    ids = expert_ids[0]
    raw = route_weight[0]
    share = raw / jnp.sum(raw, axis=0, keepdims=True)
    row = lax.broadcasted_iota(jnp.int32, (8, T), 0)
    for g in range(n):
        table = jnp.zeros((8, T), F32)
        for k in range(expert_ids.shape[1]):
            hit = (row < EL) & (row + g * EL == ids[k:k + 1, :])
            table = table + jnp.where(hit, share[k:k + 1, :], 0.0)
        tbl[g] = jnp.where(row == 7, seg_row, table)
    def rt_copy(k):
        to = lax.rem(c + k, n)
        return remote(tbl.at[to], rt.at[c], rtss.at[k - 1], rtrs.at[c], expert=to)

    x = tokens[0].astype(F32)
    scale = lax.rsqrt(jnp.mean(x * x, axis=-1, keepdims=True) + 1e-06)
    nrm[...] = (x * scale * attn_gain[...].astype(F32).reshape(1, W)).astype(BF16)
    lane = lax.broadcasted_iota(jnp.int32, (T, LANES), 1)
    for i in range(3):
        loads[i].wait()
    cosine = cosv[...]
    sine = sinv[...]
    key_cos = jnp.where(lane < 64, cosine, 1.0)
    key_lo = jnp.where(lane < 32, -sine, 0.0)
    key_hi = jnp.where((lane >= 32) & (lane < 64), sine, 0.0)
    pgw[...] = jnp.broadcast_to(page[...].astype(F32), pgw.shape)
    for h2 in range(LKV // 2):
        pair = dot(nrm[...], wkv[:, h2 * 256:(h2 + 1) * 256])
        for o in range(2):
            ch = pair[:, o * LANES:(o + 1) * LANES]
            ch = ch * key_cos + pltpu.roll(ch, 96, 1) * key_lo + pltpu.roll(ch, 32, 1) * key_hi
            kvw[0, 2 * h2 + o] = ch.astype(BF16)
    for j in range(1, win + 1):
        @pl.when(c < j)
        def _():
            kvw[j] = jnp.zeros(kvw.shape[1:], BF16)

    def dp_copy(k):
        return remote(kvw.at[0], dpr.at[k - 1], dpss.at[k - 1], dprs.at[k - 1], dp=(d + k) % nd)

    pl.semaphore_wait(barrier, (n - 1) + (nd - 1) + 1)

    steps = win // 2

    def kv_z(k, h):
        at = 2 * k + 2
        return remote(
            kvw.at[2 * k, h], kvw.at[at, h], kvzs.at[k * LKV + h], kvrs.at[(at - 1) * LKV + h],
            expert=lax.rem(c + 2, n),
        )

    def kv_y(k, h):
        to = 2 * k + 1 - 2 * y
        return remote(
            kvw.at[2 * k, h], kvw.at[to, h], kvys.at[k * LKV + h], kvrs.at[(to - 1) * LKV + h],
            expert=ypeer,
        )

    def kv_arrived(j, h):
        remote(
            kvw.at[0, h], kvw.at[j, h], kvzs.at[0], kvrs.at[(j - 1) * LKV + h], expert=ypeer
        ).wait_recv()

    def sends_z(k):
        return (z >= k) & (z + 1 < nz) & (k < steps)

    def sends_y(k):
        if k == 0:
            return y == 0
        return (z >= k) if k < steps else (z >= k) & (y == 1)

    def kv_send(k, h):
        if k < steps:
            @pl.when(sends_z(k))
            def _():
                kv_z(k, h).start()

        @pl.when(sends_y(k))
        def _():
            kv_y(k, h).start()

    for h in range(LKV):
        kv_send(0, h)

    for k in range(1, n):
        rt_copy(k).start()
    rt[c] = tbl[c]

    def pg_copy(k):
        return remote(pgw, pgr.at[k - 1], pgss.at[k - 1], pgrs.at[k - 1], dp=(d + k) % nd)

    for k in range(1, nd):
        dp_copy(k).start()
        pg_copy(k).start()

    for copy in loads[4:]:
        copy.start()

    loads[3].wait()
    q_cos = cosine * 0.125
    q_lo = jnp.where(lane % 64 < 32, -sine, 0.0) * 0.125
    q_hi = jnp.where(lane % 64 >= 32, sine, 0.0) * 0.125
    for h2 in range(qs.shape[1] // 256):
        pair = dot(nrm[...], wq[:, h2 * 256:(h2 + 1) * 256])
        for o in range(2):
            ch = pair[:, o * LANES:(o + 1) * LANES]
            ch = ch * q_cos + pltpu.roll(ch, 96, 1) * q_lo + pltpu.roll(ch, 32, 1) * q_hi
            at = h2 * 256 + o * LANES
            qs[:, at:at + LANES] = ch.astype(BF16).astype(F32)

    my_rows = pl.ds(pl.multiple_of(s * H, H), H)
    other_rows = pl.ds(pl.multiple_of((1 - s) * H, H), H)
    def rows_of(col, sec):
        return pl.ds(pl.multiple_of((col * 2 + sec) * H, H), H)

    def kv_pass(k, h):
        @pl.when(z >= k)
        def _():
            kv_arrived(2 * k, h)
        kv_send(k, h)

    for k in range(1, steps):
        for h in range(LKV):
            kv_pass(k, h)
    kv_pass(steps, 0)

    def rt_arrived(at):
        remote(tbl.at[0], rt.at[at], rtss.at[0], rtrs.at[at], expert=ypeer).wait_recv()

    for k in range(1, win + 1):
        @pl.when(c >= k)
        def _():
            rt_arrived(c - k)

    eye = lax.broadcasted_iota(jnp.int32, (T, T), 0)
    col = lax.broadcasted_iota(jnp.int32, (T, T), 1)
    seg_col = jnp.sum(jnp.where(eye == col, jnp.broadcast_to(seg_row, (T, T)), 0.0), axis=1, keepdims=True)
    for j in range(win + 1):
        seg_j = rt[jnp.where(c >= j, c - j, c), 7:8, :]
        key_pos = (c - j) * T + col
        allowed = (key_pos >= 0) & (key_pos <= c * T + eye) & (seg_j == seg_col)
        bias[:, j * T:(j + 1) * T] = jnp.where(allowed, 0.0, -1e30)

    heads = []
    keys = (win + 1) * T
    for zh in range(LKV):
        if zh + 1 < LKV:
            kv_pass(steps, zh + 1)
        for k in range(steps):
            @pl.when(c >= 2 * k + 1)
            def _():
                kv_arrived(2 * k + 1, zh)
        kv_head = kvw[:, zh].reshape(keys, LANES)
        group = []
        for m in range(G):
            h = zh * G + m
            ch = qs[:, (h // 2) * LANES:(h // 2 + 1) * LANES]
            if h % 2:
                ch = pltpu.roll(ch, 64, 1)
            group.append(jnp.where(lane < 64, ch, 0.0).astype(BF16))
        q3 = jnp.concatenate(group, axis=0)
        score = lax.dot_general(q3, kv_head, (((1,), (1,)), ((), ())), preferred_element_type=F32)
        score = score.reshape(G, T, keys) + bias[...][None]
        top = jnp.max(score, axis=-1, keepdims=True)
        unscaled = jnp.exp(score - top)
        count = jnp.sum(unscaled, axis=-1, keepdims=True)
        weighted = dot(unscaled.astype(BF16).reshape(G * T, keys), kv_head).reshape(G, T, LANES)
        weighted = weighted / count
        for m in range(G):
            heads.append(weighted[m])
            if len(heads) == 2:
                k = (zh * G + m) // 2
                both = jnp.where(lane < 64, pltpu.roll(heads[0], 64, 1), heads[1])
                attd[:, k * LANES:(k + 1) * LANES] = both.astype(BF16)
                heads = []

    loads[4].wait()
    for k in range(W // 256):
        hp[:, k * 256:(k + 1) * 256] = dot(attd[...], wo[:, k * 256:(k + 1) * 256])
    hps[...] = hp[other_rows, :].astype(BF16)
    head_copy = remote(hps, hpr, hsem.at[0], hsem.at[1], section=1 - s)
    head_copy.start()

    for k in range(1, nd):
        dp_copy(k).wait_recv()
        pg_copy(k).wait_recv()
    target = (d * n + c).astype(F32)
    own_id = pgw[0:1, 0:1]
    for h in range(LKV):
        picked = jnp.where(own_id == target, kvw[0, h].astype(F32), 0.0)
        for k in range(1, nd):
            picked = jnp.where(pgr[k - 1, 0:1, 0:1] == target, dpr[k - 1, h].astype(F32), picked)
        cache[0, :, h * LANES:(h + 1) * LANES] = picked.astype(BF16)

    head_copy.wait_recv()
    resid = tokens[0, my_rows, :].astype(F32) + (hp[my_rows, :] + hpr[...].astype(F32))
    rs[...] = resid
    scale = lax.rsqrt(jnp.mean(resid * resid, axis=-1, keepdims=True) + 1e-06)
    mb[rows_of(c, s), :] = (resid * scale * ffn_gain[...].astype(F32).reshape(1, W)).astype(BF16)

    CH = GATHER_CHUNKS
    HR = H // CH

    def mb_copy(colm, sec, h, ss, **dev):
        rows = pl.ds(pl.multiple_of((colm * 2 + sec) * H + h * HR, HR), HR)
        return remote(mb.at[rows], mb.at[rows], ss, mbrs.at[(colm * 2 + sec) * CH + h], **dev)

    def up_copy(zi, h):
        return mb_copy(zi * 2 + y, s, h, ups.at[zi * CH + h], expert=lax.rem(c + 2, n))

    def down_copy(zi, h):
        return mb_copy(zi * 2 + y, s, h, downs.at[zi * CH + h], expert=lax.rem(c + n - 2, n))

    def y_copy(zi, h):
        return mb_copy(zi * 2 + y, s, h, yss.at[zi * CH + h], expert=ypeer)

    def p_copy(colm, h):
        return mb_copy(colm, s, h, pss.at[colm * CH + h], section=1 - s)

    for h in range(CH):
        @pl.when(z + 1 < nz)
        def _():
            up_copy(z, h).start()

        @pl.when(z >= 1)
        def _():
            down_copy(z, h).start()

        if h < CH // 2:
            y_copy(z, h).start()
        p_copy(c, h).start()
    other_half = pl.ds(pl.multiple_of((1 - s) * HW, HW), HW)
    my_half = pl.ds(pl.multiple_of(s * HW, HW), HW)
    resid_copy = remote(rs.at[:, other_half], rr, rsem_r.at[0], rsem_r.at[1], section=1 - s)
    resid_copy.start()
    for i in range(5, 8):
        loads[i].wait()

    def sec_copy(i, p):
        at = 2 * i + p
        return remote(secs.at[at], secr.at[at], secss.at[at], secrs.at[at], section=1 - s)

    def yr_copy(i, p):
        at = 2 * i + p
        return remote(ysnd.at[at], yrcv.at[at], yrss.at[at], yrrs.at[at], expert=ypeer)

    def zr_copy(zi, p):
        at, to = 2 * zi + p, 2 * z + p
        return remote(zsnd.at[at], zrcv.at[to], zrss.at[at], zrrs.at[to], expert=zi * 2 + y)

    def zr_arrived(zi, p):
        at = 2 * zi + p
        remote(zsnd.at[at], zrcv.at[at], zrss.at[at], zrrs.at[at], expert=zi * 2 + y).wait_recv()

    def near(b):
        return (b == z + 1) | (b == z - 1)

    def near_copy(b, p):
        at = jnp.where(b > z, 0, 2) + p
        return remote(ns.at[at], nr.at[at], nss.at[at], nrs.at[at], expert=b * 2 + y)

    def near_arrived(at):
        remote(ns.at[at], nr.at[at], nss.at[at], nrs.at[at], expert=ypeer).wait_recv()

    def fy_copy(p):
        return remote(fys.at[p], fyr.at[p], fyss.at[p], fyrs.at[p], expert=ypeer)

    to_peer = pl.ds(pl.multiple_of((1 - y) * T, T), T)
    kept = pl.ds(pl.multiple_of(y * T, T), T)

    def layer_of(j):
        k = (j + 1) // 2
        return z + k * (1 - 2 * (j % 2))

    def exists(j):
        return (layer_of(j) >= 0) & (layer_of(j) < nz)

    def pass_on(j):
        zi = layer_of(j)

        @pl.when(exists(j) & (j < 2 * nz - 1))
        def _():
            for h in range(CH):
                mb_copy(zi * 2 + y, s, h, pss.at[0], section=1 - s).wait_recv()

                @pl.when((zi < z) & (z + 1 < nz))
                def _():
                    up_copy(zi, h).start()

                @pl.when((zi > z) & (z >= 1))
                def _():
                    down_copy(zi, h).start()

                y_copy(zi, h).start()
                p_copy(zi * 2 + y, h).start()

    pass_on(1)
    pass_on(2)
    for j in range(3, min(5, 2 * nz - 1)):
        pass_on(j)
    for h in range(CH // 2, CH):
        y_copy(z, h).start()
    for k in range(1, n):
        @pl.when((c < k) | (k > win))
        def _():
            rt_arrived(lax.rem(c + n - k, n))

    def far_return(j, also):
        @pl.when(exists(j) & also)
        def _():
            b = layer_of(j)
            for p in range(2):
                at = 2 * b + p
                yr_copy(b, p).wait_recv()
                zsnd[at] = (sown[at] + yrcv[at].astype(F32)).astype(BF16)
                zr_copy(b, p).start()

    def late_step(j, carry):
        far_return(j, (j + 2 > 2 * nz - 2) | ~exists(j + 2))
        return carry

    def step(turn, carry):
        j = lax.rem(turn + 1, 2 * nz - 1)

        @pl.when(exists(j))
        def _():
            zi = layer_of(j)
            theirs = zi * 2 + (1 - y)
            for h in range(CH):
                mb_copy(theirs, s, h, pss.at[0], section=1 - s).wait_recv()
                p_copy(theirs, h).start()
            for h in range(CH):
                mb_copy(zi * 2 + y, 1 - s, h, pss.at[0], section=1 - s).wait_recv()
            for h in range(CH):
                mb_copy(theirs, 1 - s, h, pss.at[0], section=1 - s).wait_recv()
            rows = pl.ds(pl.multiple_of(zi * (2 * T), 2 * T), 2 * T)
            shares = jnp.concatenate([rt[2 * zi].T, rt[2 * zi + 1].T], axis=0)
            for e in range(EL):
                share_e = shares[:, e:e + 1]
                gate = dot(mb[rows, :], wg[e])
                up = dot(mb[rows, :], wu[e])
                activ = gate / (1.0 + jnp.exp(-gate)) * up
                act[:, e * FL:(e + 1) * FL] = (activ * share_e).astype(BF16)
            for p in range(2):
                cols = pl.ds(pl.multiple_of((1 - s) * HW + p * PW, LANES), PW)
                secs[2 * zi + p] = dot(act[...], wd[:, cols]).astype(BF16)
                sec_copy(zi, p).start()

        far_return(j - 2, (j >= 5) & exists(j))
        pass_on(turn + 5)

        @pl.when(exists(j))
        def _():
            b = layer_of(j)
            for p in range(2):
                at = 2 * b + p
                cols = pl.ds(pl.multiple_of(s * HW + p * PW, LANES), PW)
                mine[at] = dot(act[...], wd[:, cols])
                sec_copy(b, p).wait_recv()

                @pl.when(b == z)
                def _():
                    mine[at] = mine[at] + secr[at].astype(F32)

                @pl.when(near(b))
                def _():
                    to = jnp.where(b > z, 0, 2) + p
                    ns[to] = (mine[at] + secr[at].astype(F32)).astype(BF16)
                    near_copy(b, p).start()

                @pl.when((b != z) & ~near(b))
                def _():
                    ysnd[at] = (mine[at, to_peer, :] + secr[at, to_peer, :].astype(F32)).astype(BF16)
                    yr_copy(b, p).start()
                    sown[at] = mine[at, kept, :] + secr[at, kept, :].astype(F32)

        return carry

    lax.fori_loop(0, 2 * nz - 1, step, 0)

    lax.fori_loop(3, min(5, 2 * nz - 1), late_step, 0)

    for p in range(2):
        for side in range(2):
            @pl.when((z >= 1) if side == 0 else (z + 1 < nz))
            def _():
                near_arrived(2 * side + p)
                mine[2 * z + p] = mine[2 * z + p] + nr[2 * side + p].astype(F32)

        fys[p] = mine[2 * z + p, to_peer, :].astype(BF16)
        fy_copy(p).start()

    lax.fori_loop(5, 2 * nz - 1, late_step, 0)
    resid_copy.wait_recv()
    for p in range(2):
        fy_copy(p).wait_recv()
        sown[2 * z + p] = mine[2 * z + p, kept, :] + fyr[p].astype(F32)

        def far_sum(k, carry):
            zi = lax.rem(z + k, nz)

            @pl.when(~near(zi))
            def _():
                zr_arrived(zi, p)
                sown[2 * z + p] = sown[2 * z + p] + zrcv[2 * zi + p].astype(F32)

            return carry

        lax.fori_loop(1, nz, far_sum, 0)
        cols = slice(p * PW, (p + 1) * PW)
        at = pl.ds(pl.multiple_of(s * HW + p * PW, LANES), PW)
        out[0, my_rows, cols] = (rs[:, at] + sown[2 * z + p, my_rows, :]).astype(BF16)
        out[0, other_rows, cols] = (rr[:, cols] + sown[2 * z + p, other_rows, :]).astype(BF16)

    for p in range(2):
        fy_copy(p).wait_send()
    for k in range(1, n):
        rt_copy(k).wait_send()

    for h in range(LKV):
        for k in range(steps + 1):
            if k < steps:
                @pl.when(sends_z(k))
                def _():
                    kv_z(k, h).wait_send()

            @pl.when(sends_y(k))
            def _():
                kv_y(k, h).wait_send()
    for k in range(1, nd):
        dp_copy(k).wait_send()
        pg_copy(k).wait_send()
    head_copy.wait_send()
    resid_copy.wait_send()
    for zi in range(nz):
        for h in range(CH):
            @pl.when((zi <= z) & (z + 1 < nz))
            def _():
                up_copy(zi, h).wait_send()

            @pl.when((zi >= z) & (z >= 1))
            def _():
                down_copy(zi, h).wait_send()

            y_copy(zi, h).wait_send()
            p_copy(2 * zi, h).wait_send()
            p_copy(2 * zi + 1, h).wait_send()

        for p in range(2):
            @pl.when(near(zi))
            def _():
                near_copy(zi, p).wait_send()

            @pl.when((zi != z) & ~near(zi))
            def _():
                yr_copy(zi, p).wait_send()
                zr_copy(zi, p).wait_send()

        for p in range(2):
            sec_copy(zi, p).wait_send()


def trig(count):
    half = HEAD_WIDTH // 2
    frequency = np.float32(10000.0) ** (
        -(np.arange(half, dtype=np.float32) * np.float32(2.0) / np.float32(HEAD_WIDTH))
    )
    angles = np.arange(count, dtype=np.float32)[:, None] * frequency.astype(np.float32)[None, :]
    reps = LANES // half
    wide = np.tile(angles.astype(np.float64), (1, reps))
    return np.cos(wide).astype(np.float32), np.sin(wide).astype(np.float32)


def shards(
    tokens, segments, attn_gain, query_weight, key_value_weight, out_weight, ffn_gain,
    gate_weight, up_weight, down_weight, expert_ids, route_weight, stream_page_table,
):
    n = lax.axis_size("expert")
    nd = lax.axis_size("dp")
    win = n // 2
    nz = n // 2
    T, W = tokens.shape[1], tokens.shape[2]
    H, HW = T // 2, W // 2
    EL, _, FL = gate_weight.shape
    qw, kw = query_weight.shape[1], key_value_weight.shape[1]
    cosine, sine = trig(T * n)
    down = down_weight.reshape(EL * FL, W)
    vmem = pl.BlockSpec(memory_space=pltpu.VMEM)
    hbm = pl.BlockSpec(memory_space=pl.ANY)
    dma = pltpu.SemaphoreType.DMA
    out, cache = pl.pallas_call(
        functools.partial(layer_kernel, n, nd, win),
        out_shape=(
            jax.ShapeDtypeStruct((1, T, HW), BF16),
            jax.ShapeDtypeStruct((1, T, kw), BF16),
        ),
        in_specs=[vmem] * 7 + [hbm] * 8,
        out_specs=(vmem, vmem),
        scratch_shapes=[
            pltpu.VMEM((W, qw), BF16),
            pltpu.VMEM((W, kw), BF16),
            pltpu.VMEM((qw, W), BF16),
            pltpu.VMEM((EL, W, FL), BF16),
            pltpu.VMEM((EL, W, FL), BF16),
            pltpu.VMEM((EL * FL, W), BF16),
            pltpu.VMEM((T, LANES), F32),
            pltpu.VMEM((T, LANES), F32),
            pltpu.VMEM((n, 8, T), F32),
            pltpu.VMEM((n, 8, T), F32),
            pltpu.VMEM((T, W), BF16),
            pltpu.VMEM((win + 1, kw // LANES, T, LANES), BF16),
            pltpu.VMEM((nd - 1, kw // LANES, T, LANES), BF16),
            pltpu.VMEM((8, LANES), F32),
            pltpu.VMEM((nd - 1, 8, LANES), F32),
            pltpu.VMEM((T, qw), F32),
            pltpu.VMEM((T, (win + 1) * T), F32),
            pltpu.VMEM((T, qw), BF16),
            pltpu.VMEM((T, W), F32),
            pltpu.VMEM((H, W), BF16),
            pltpu.VMEM((H, W), BF16),
            pltpu.VMEM((H, W), F32),
            pltpu.VMEM((H, HW), F32),
            pltpu.VMEM((n * T, W), BF16),
            pltpu.VMEM((2 * T, EL * FL), BF16),
            pltpu.VMEM((2 * nz, 2 * T, HW // 2), BF16),
            pltpu.VMEM((2 * nz, 2 * T, HW // 2), BF16),
            pltpu.VMEM((2 * nz, 2 * T, HW // 2), F32),
            pltpu.VMEM((2 * nz, T, HW // 2), BF16),
            pltpu.VMEM((2 * nz, T, HW // 2), BF16),
            pltpu.VMEM((2 * nz, T, HW // 2), F32),
            pltpu.VMEM((2 * nz, T, HW // 2), BF16),
            pltpu.VMEM((2 * nz, T, HW // 2), BF16),
            pltpu.VMEM((4, 2 * T, HW // 2), BF16),
            pltpu.VMEM((4, 2 * T, HW // 2), BF16),
            pltpu.VMEM((2, T, HW // 2), BF16),
            pltpu.VMEM((2, T, HW // 2), BF16),
            dma((8,)),
            dma((win // 2 * (kw // LANES),)), dma(((win // 2 + 1) * (kw // LANES),)), dma((win * (kw // LANES),)),
            dma((nd - 1,)), dma((nd - 1,)), dma((nd - 1,)), dma((nd - 1,)),
            dma((2,)), dma((2,)),
            dma((nz * GATHER_CHUNKS,)), dma((nz * GATHER_CHUNKS,)), dma((nz * GATHER_CHUNKS,)),
            dma((n * GATHER_CHUNKS,)), dma((2 * n * GATHER_CHUNKS,)),
            dma((n,)), dma((n,)), dma((n,)), dma((n,)), dma((n,)), dma((n,)),
            dma((4,)), dma((4,)), dma((2,)), dma((2,)), dma((n,)), dma((n,)),
        ],
        compiler_params=pltpu.CompilerParams(
            collective_id=0, has_side_effects=True, vmem_limit_bytes=58 * 1024 * 1024
        ),
    )(
        tokens, segments, attn_gain, ffn_gain, expert_ids.transpose(0, 2, 1),
        route_weight.transpose(0, 2, 1), stream_page_table, jnp.asarray(cosine), jnp.asarray(sine),
        query_weight, key_value_weight, out_weight, gate_weight, up_weight, down,
    )

    def hand_over(out_in, cache_in, out_to, cache_to):
        out_to[...] = out_in[...]
        cache_to[...] = cache_in[...]

    return pl.pallas_call(
        hand_over,
        out_shape=(jax.ShapeDtypeStruct(out.shape, BF16), jax.ShapeDtypeStruct(cache.shape, BF16)),
        in_specs=[vmem, vmem],
        out_specs=(vmem, vmem),
    )(out, cache)


def solution(mesh):
    in_specs = (
        P("dp", "expert", None),
        P("dp", "expert"),
        P(),
        P(None, "section"),
        P(None, "section"),
        P("section", None),
        P(),
        P("expert", None, "section"),
        P("expert", None, "section"),
        P("expert", "section", None),
        P("dp", "expert", None),
        P("dp", "expert", None),
        P("dp", "expert"),
    )
    out_specs = (P("dp", "expert", "section"), P(("dp", "expert"), None, "section"))
    return jax.shard_map(shards, mesh=mesh, in_specs=in_specs, out_specs=out_specs, check_vma=False)
```

```python
import functools
import math

import jax
import jax.numpy as jnp
import numpy as np
from jax import lax
from jax.experimental import pallas as pl
from jax.experimental.pallas import tpu as pltpu
from jax.sharding import PartitionSpec as P

QUERY_HEADS = 24
KEYVALUE_HEADS = 8
HEAD_WIDTH = 64
LANES = 128
GATHER_CHUNKS = 2
MESH = pl.DeviceIdType.MESH
F32 = jnp.float32
BF16 = jnp.bfloat16


def dot(a, b):
    return jnp.dot(a, b, preferred_element_type=F32)


def layer_kernel(
    n, nd, win,
    tokens, segments, attn_gain, ffn_gain, expert_ids, route_weight, page,
    cos_hbm, sin_hbm, wq_hbm, wkv_hbm, wo_hbm, wg_hbm, wu_hbm, wd_hbm,
    out, cache,
    wq, wkv, wo, wg, wu, wd, cosv, sinv,
    tbl, rt, nrm, kvw, dpr, pgw, pgr, qs, bias, attd, hp, hps, hpr, rs, rr, mb,
    act, secs, secr, mine, ysnd, yrcv, sown, zsnd, zrcv, ns, nr, fys, fyr,
    wsem, kvzs, kvys, kvrs, dpss, dprs, pgss, pgrs, hsem, rsem_r, ups, downs, yss, pss, mbrs,
    secss, secrs, yrss, yrrs, zrss, zrrs, nss, nrs, fyss, fyrs, rtss, rtrs,
):
    s = lax.axis_index("section")
    d = lax.axis_index("dp")
    c = lax.axis_index("expert")
    nz = n // 2
    z = c // 2
    y = c % 2
    T = tokens.shape[1]
    H = T // 2
    W = tokens.shape[2]
    HW = W // 2
    PW = HW // 2
    EL = wg.shape[0]
    FL = wg.shape[2]
    LKV = wkv.shape[1] // LANES
    G = QUERY_HEADS // KEYVALUE_HEADS
    ypeer = z * 2 + (1 - y)

    def local(src, dst, i):
        return pltpu.make_async_copy(src, dst, wsem.at[i])

    loads = [
        local(wkv_hbm, wkv, 0),
        local(cos_hbm.at[pl.ds(pl.multiple_of(c * T, T), T)], cosv, 1),
        local(sin_hbm.at[pl.ds(pl.multiple_of(c * T, T), T)], sinv, 2),
        local(wq_hbm, wq, 3),
        local(wo_hbm, wo, 4),
        local(wg_hbm, wg, 5),
        local(wu_hbm, wu, 6),
        local(wd_hbm, wd, 7),
    ]
    for copy in loads[:4]:
        copy.start()

    barrier = pltpu.get_barrier_semaphore()
    for k in range(1, n):
        pl.semaphore_signal(barrier, inc=1, device_id={"expert": (c + k) % n}, device_id_type=MESH)
    for k in range(1, nd):
        pl.semaphore_signal(barrier, inc=1, device_id={"dp": (d + k) % nd}, device_id_type=MESH)
    pl.semaphore_signal(barrier, inc=1, device_id={"section": 1 - s}, device_id_type=MESH)

    def remote(src, dst, ss, rsm, **dev):
        return pltpu.make_async_remote_copy(
            src_ref=src, dst_ref=dst, send_sem=ss, recv_sem=rsm, device_id=dev, device_id_type=MESH
        )

    seg_row = segments[...].astype(F32)
    ids = expert_ids[0]
    raw = route_weight[0]
    share = raw / jnp.sum(raw, axis=0, keepdims=True)
    row = lax.broadcasted_iota(jnp.int32, (8, T), 0)
    for g in range(n):
        table = jnp.zeros((8, T), F32)
        for k in range(expert_ids.shape[1]):
            hit = (row < EL) & (row + g * EL == ids[k:k + 1, :])
            table = table + jnp.where(hit, share[k:k + 1, :], 0.0)
        tbl[g] = jnp.where(row == 7, seg_row, table)
    def rt_copy(k):
        to = lax.rem(c + k, n)
        return remote(tbl.at[to], rt.at[c], rtss.at[k - 1], rtrs.at[c], expert=to)

    x = tokens[0].astype(F32)
    scale = lax.rsqrt(jnp.mean(x * x, axis=-1, keepdims=True) + 1e-06)
    nrm[...] = (x * scale * attn_gain[...].astype(F32).reshape(1, W)).astype(BF16)
    lane = lax.broadcasted_iota(jnp.int32, (T, LANES), 1)
    for i in range(3):
        loads[i].wait()
    cosine = cosv[...]
    sine = sinv[...]
    key_cos = jnp.where(lane < 64, cosine, 1.0)
    key_lo = jnp.where(lane < 32, -sine, 0.0)
    key_hi = jnp.where((lane >= 32) & (lane < 64), sine, 0.0)
    pgw[...] = jnp.broadcast_to(page[...].astype(F32), pgw.shape)
    for h2 in range(LKV // 2):
        pair = dot(nrm[...], wkv[:, h2 * 256:(h2 + 1) * 256])
        for o in range(2):
            ch = pair[:, o * LANES:(o + 1) * LANES]
            ch = ch * key_cos + pltpu.roll(ch, 96, 1) * key_lo + pltpu.roll(ch, 32, 1) * key_hi
            kvw[0, 2 * h2 + o] = ch.astype(BF16)
    for j in range(1, win + 1):
        @pl.when(c < j)
        def _():
            kvw[j] = jnp.zeros(kvw.shape[1:], BF16)

    def dp_copy(k):
        return remote(kvw.at[0], dpr.at[k - 1], dpss.at[k - 1], dprs.at[k - 1], dp=(d + k) % nd)

    pl.semaphore_wait(barrier, (n - 1) + (nd - 1) + 1)

    steps = win // 2

    def kv_z(k, h):
        at = 2 * k + 2
        return remote(
            kvw.at[2 * k, h], kvw.at[at, h], kvzs.at[k * LKV + h], kvrs.at[(at - 1) * LKV + h],
            expert=lax.rem(c + 2, n),
        )

    def kv_y(k, h):
        to = 2 * k + 1 - 2 * y
        return remote(
            kvw.at[2 * k, h], kvw.at[to, h], kvys.at[k * LKV + h], kvrs.at[(to - 1) * LKV + h],
            expert=ypeer,
        )

    def kv_arrived(j, h):
        remote(
            kvw.at[0, h], kvw.at[j, h], kvzs.at[0], kvrs.at[(j - 1) * LKV + h], expert=ypeer
        ).wait_recv()

    def sends_z(k):
        return (z >= k) & (z + 1 < nz) & (k < steps)

    def sends_y(k):
        if k == 0:
            return y == 0
        return (z >= k) if k < steps else (z >= k) & (y == 1)

    def kv_send(k, h):
        if k < steps:
            @pl.when(sends_z(k))
            def _():
                kv_z(k, h).start()

        @pl.when(sends_y(k))
        def _():
            kv_y(k, h).start()

    for h in range(LKV):
        kv_send(0, h)

    for k in range(1, n):
        rt_copy(k).start()
    rt[c] = tbl[c]

    def pg_copy(k):
        return remote(pgw, pgr.at[k - 1], pgss.at[k - 1], pgrs.at[k - 1], dp=(d + k) % nd)

    for k in range(1, nd):
        dp_copy(k).start()
        pg_copy(k).start()

    for copy in loads[4:]:
        copy.start()

    loads[3].wait()
    q_cos = cosine * 0.125
    q_lo = jnp.where(lane % 64 < 32, -sine, 0.0) * 0.125
    q_hi = jnp.where(lane % 64 >= 32, sine, 0.0) * 0.125
    for h2 in range(qs.shape[1] // 256):
        pair = dot(nrm[...], wq[:, h2 * 256:(h2 + 1) * 256])
        for o in range(2):
            ch = pair[:, o * LANES:(o + 1) * LANES]
            ch = ch * q_cos + pltpu.roll(ch, 96, 1) * q_lo + pltpu.roll(ch, 32, 1) * q_hi
            at = h2 * 256 + o * LANES
            qs[:, at:at + LANES] = ch.astype(BF16).astype(F32)

    my_rows = pl.ds(pl.multiple_of(s * H, H), H)
    other_rows = pl.ds(pl.multiple_of((1 - s) * H, H), H)
    def rows_of(col, sec):
        return pl.ds(pl.multiple_of((col * 2 + sec) * H, H), H)

    def kv_pass(k, h):
        @pl.when(z >= k)
        def _():
            kv_arrived(2 * k, h)
        kv_send(k, h)

    for k in range(1, steps):
        for h in range(LKV):
            kv_pass(k, h)
    kv_pass(steps, 0)

    def rt_arrived(at):
        remote(tbl.at[0], rt.at[at], rtss.at[0], rtrs.at[at], expert=ypeer).wait_recv()

    for k in range(1, win + 1):
        @pl.when(c >= k)
        def _():
            rt_arrived(c - k)

    eye = lax.broadcasted_iota(jnp.int32, (T, T), 0)
    col = lax.broadcasted_iota(jnp.int32, (T, T), 1)
    seg_col = jnp.sum(jnp.where(eye == col, jnp.broadcast_to(seg_row, (T, T)), 0.0), axis=1, keepdims=True)
    for j in range(win + 1):
        seg_j = rt[jnp.where(c >= j, c - j, c), 7:8, :]
        key_pos = (c - j) * T + col
        allowed = (key_pos >= 0) & (key_pos <= c * T + eye) & (seg_j == seg_col)
        bias[:, j * T:(j + 1) * T] = jnp.where(allowed, 0.0, -1e30)

    heads = []
    keys = (win + 1) * T
    for zh in range(LKV):
        if zh + 1 < LKV:
            kv_pass(steps, zh + 1)
        for k in range(steps):
            @pl.when(c >= 2 * k + 1)
            def _():
                kv_arrived(2 * k + 1, zh)
        kv_head = kvw[:, zh].reshape(keys, LANES)
        group = []
        for m in range(G):
            h = zh * G + m
            ch = qs[:, (h // 2) * LANES:(h // 2 + 1) * LANES]
            if h % 2:
                ch = pltpu.roll(ch, 64, 1)
            group.append(jnp.where(lane < 64, ch, 0.0).astype(BF16))
        q3 = jnp.concatenate(group, axis=0)
        score = lax.dot_general(q3, kv_head, (((1,), (1,)), ((), ())), preferred_element_type=F32)
        score = score.reshape(G, T, keys) + bias[...][None]
        top = jnp.max(score, axis=-1, keepdims=True)
        unscaled = jnp.exp(score - top)
        count = jnp.sum(unscaled, axis=-1, keepdims=True)
        weighted = dot(unscaled.astype(BF16).reshape(G * T, keys), kv_head).reshape(G, T, LANES)
        weighted = weighted / count
        for m in range(G):
            heads.append(weighted[m])
            if len(heads) == 2:
                k = (zh * G + m) // 2
                both = jnp.where(lane < 64, pltpu.roll(heads[0], 64, 1), heads[1])
                attd[:, k * LANES:(k + 1) * LANES] = both.astype(BF16)
                heads = []

    loads[4].wait()
    for k in range(W // 256):
        hp[:, k * 256:(k + 1) * 256] = dot(attd[...], wo[:, k * 256:(k + 1) * 256])
    hps[...] = hp[other_rows, :].astype(BF16)
    head_copy = remote(hps, hpr, hsem.at[0], hsem.at[1], section=1 - s)
    head_copy.start()

    for k in range(1, nd):
        dp_copy(k).wait_recv()
        pg_copy(k).wait_recv()
    target = (d * n + c).astype(F32)
    own_id = pgw[0:1, 0:1]
    for h in range(LKV):
        picked = jnp.where(own_id == target, kvw[0, h].astype(F32), 0.0)
        for k in range(1, nd):
            picked = jnp.where(pgr[k - 1, 0:1, 0:1] == target, dpr[k - 1, h].astype(F32), picked)
        cache[0, :, h * LANES:(h + 1) * LANES] = picked.astype(BF16)

    head_copy.wait_recv()
    resid = tokens[0, my_rows, :].astype(F32) + (hp[my_rows, :] + hpr[...].astype(F32))
    rs[...] = resid
    scale = lax.rsqrt(jnp.mean(resid * resid, axis=-1, keepdims=True) + 1e-06)
    mb[rows_of(c, s), :] = (resid * scale * ffn_gain[...].astype(F32).reshape(1, W)).astype(BF16)

    CH = GATHER_CHUNKS
    HR = H // CH

    def mb_copy(colm, sec, h, ss, **dev):
        rows = pl.ds(pl.multiple_of((colm * 2 + sec) * H + h * HR, HR), HR)
        return remote(mb.at[rows], mb.at[rows], ss, mbrs.at[(colm * 2 + sec) * CH + h], **dev)

    def up_copy(zi, h):
        return mb_copy(zi * 2 + y, s, h, ups.at[zi * CH + h], expert=lax.rem(c + 2, n))

    def down_copy(zi, h):
        return mb_copy(zi * 2 + y, s, h, downs.at[zi * CH + h], expert=lax.rem(c + n - 2, n))

    def y_copy(zi, h):
        return mb_copy(zi * 2 + y, s, h, yss.at[zi * CH + h], expert=ypeer)

    def p_copy(colm, h):
        return mb_copy(colm, s, h, pss.at[colm * CH + h], section=1 - s)

    for h in range(CH):
        @pl.when(z + 1 < nz)
        def _():
            up_copy(z, h).start()

        @pl.when(z >= 1)
        def _():
            down_copy(z, h).start()

        if h < CH // 2:
            y_copy(z, h).start()
        p_copy(c, h).start()
    other_half = pl.ds(pl.multiple_of((1 - s) * HW, HW), HW)
    my_half = pl.ds(pl.multiple_of(s * HW, HW), HW)
    resid_copy = remote(rs.at[:, other_half], rr, rsem_r.at[0], rsem_r.at[1], section=1 - s)
    resid_copy.start()
    for i in range(5, 8):
        loads[i].wait()

    def sec_copy(i, p):
        at = 2 * i + p
        return remote(secs.at[at], secr.at[at], secss.at[at], secrs.at[at], section=1 - s)

    def yr_copy(i, p):
        at = 2 * i + p
        return remote(ysnd.at[at], yrcv.at[at], yrss.at[at], yrrs.at[at], expert=ypeer)

    def zr_copy(zi, p):
        at, to = 2 * zi + p, 2 * z + p
        return remote(zsnd.at[at], zrcv.at[to], zrss.at[at], zrrs.at[to], expert=zi * 2 + y)

    def zr_arrived(zi, p):
        at = 2 * zi + p
        remote(zsnd.at[at], zrcv.at[at], zrss.at[at], zrrs.at[at], expert=zi * 2 + y).wait_recv()

    def near(b):
        return (b == z + 1) | (b == z - 1)

    def near_copy(b, p):
        at = jnp.where(b > z, 0, 2) + p
        return remote(ns.at[at], nr.at[at], nss.at[at], nrs.at[at], expert=b * 2 + y)

    def near_arrived(at):
        remote(ns.at[at], nr.at[at], nss.at[at], nrs.at[at], expert=ypeer).wait_recv()

    def fy_copy(p):
        return remote(fys.at[p], fyr.at[p], fyss.at[p], fyrs.at[p], expert=ypeer)

    to_peer = pl.ds(pl.multiple_of((1 - y) * T, T), T)
    kept = pl.ds(pl.multiple_of(y * T, T), T)

    def layer_of(j):
        k = (j + 1) // 2
        return z + k * (1 - 2 * (j % 2))

    def exists(j):
        return (layer_of(j) >= 0) & (layer_of(j) < nz)

    def pass_on(j):
        zi = layer_of(j)

        @pl.when(exists(j) & (j < 2 * nz - 1))
        def _():
            for h in range(CH):
                mb_copy(zi * 2 + y, s, h, pss.at[0], section=1 - s).wait_recv()

                @pl.when((zi < z) & (z + 1 < nz))
                def _():
                    up_copy(zi, h).start()

                @pl.when((zi > z) & (z >= 1))
                def _():
                    down_copy(zi, h).start()

                y_copy(zi, h).start()
                p_copy(zi * 2 + y, h).start()

    pass_on(1)
    pass_on(2)
    for j in range(3, min(5, 2 * nz - 1)):
        pass_on(j)
    for h in range(CH // 2, CH):
        y_copy(z, h).start()
    for k in range(1, n):
        @pl.when((c < k) | (k > win))
        def _():
            rt_arrived(lax.rem(c + n - k, n))

    def far_return(j, also):
        @pl.when(exists(j) & also)
        def _():
            b = layer_of(j)
            for p in range(2):
                at = 2 * b + p
                yr_copy(b, p).wait_recv()
                zsnd[at] = (sown[at] + yrcv[at].astype(F32)).astype(BF16)
                zr_copy(b, p).start()

    def late_step(j, carry):
        far_return(j, (j + 2 > 2 * nz - 2) | ~exists(j + 2))
        return carry

    def step(turn, carry):
        j = lax.rem(turn + 1, 2 * nz - 1)

        @pl.when(exists(j))
        def _():
            zi = layer_of(j)
            theirs = zi * 2 + (1 - y)
            for h in range(CH):
                mb_copy(theirs, s, h, pss.at[0], section=1 - s).wait_recv()
                p_copy(theirs, h).start()
            for h in range(CH):
                mb_copy(zi * 2 + y, 1 - s, h, pss.at[0], section=1 - s).wait_recv()
            for h in range(CH):
                mb_copy(theirs, 1 - s, h, pss.at[0], section=1 - s).wait_recv()
            rows = pl.ds(pl.multiple_of(zi * (2 * T), 2 * T), 2 * T)
            shares = jnp.concatenate([rt[2 * zi].T, rt[2 * zi + 1].T], axis=0)
            for e in range(EL):
                share_e = shares[:, e:e + 1]
                gate = dot(mb[rows, :], wg[e])
                up = dot(mb[rows, :], wu[e])
                activ = gate / (1.0 + jnp.exp(-gate)) * up
                act[:, e * FL:(e + 1) * FL] = (activ * share_e).astype(BF16)
            for p in range(2):
                cols = pl.ds(pl.multiple_of((1 - s) * HW + p * PW, LANES), PW)
                secs[2 * zi + p] = dot(act[...], wd[:, cols]).astype(BF16)
                sec_copy(zi, p).start()

        far_return(j - 2, (j >= 5) & exists(j))
        pass_on(turn + 5)

        @pl.when(exists(j))
        def _():
            b = layer_of(j)
            for p in range(2):
                at = 2 * b + p
                cols = pl.ds(pl.multiple_of(s * HW + p * PW, LANES), PW)
                mine[at] = dot(act[...], wd[:, cols])
                sec_copy(b, p).wait_recv()

                @pl.when(b == z)
                def _():
                    mine[at] = mine[at] + secr[at].astype(F32)

                @pl.when(near(b))
                def _():
                    to = jnp.where(b > z, 0, 2) + p
                    ns[to] = (mine[at] + secr[at].astype(F32)).astype(BF16)
                    near_copy(b, p).start()

                @pl.when((b != z) & ~near(b))
                def _():
                    ysnd[at] = (mine[at, to_peer, :] + secr[at, to_peer, :].astype(F32)).astype(BF16)
                    yr_copy(b, p).start()

            @pl.when((b != z) & ~near(b))
            def _():
                for p in range(2):
                    at = 2 * b + p
                    sown[at] = mine[at, kept, :] + secr[at, kept, :].astype(F32)

        return carry

    lax.fori_loop(0, 2 * nz - 1, step, 0)

    lax.fori_loop(3, min(5, 2 * nz - 1), late_step, 0)

    for p in range(2):
        for side in range(2):
            @pl.when((z >= 1) if side == 0 else (z + 1 < nz))
            def _():
                near_arrived(2 * side + p)
                mine[2 * z + p] = mine[2 * z + p] + nr[2 * side + p].astype(F32)

        fys[p] = mine[2 * z + p, to_peer, :].astype(BF16)
        fy_copy(p).start()

    lax.fori_loop(5, 2 * nz - 1, late_step, 0)
    resid_copy.wait_recv()
    for p in range(2):
        fy_copy(p).wait_recv()
        sown[2 * z + p] = mine[2 * z + p, kept, :] + fyr[p].astype(F32)

        def far_sum(k, carry):
            zi = lax.rem(z + k, nz)

            @pl.when(~near(zi))
            def _():
                zr_arrived(zi, p)
                sown[2 * z + p] = sown[2 * z + p] + zrcv[2 * zi + p].astype(F32)

            return carry

        lax.fori_loop(1, nz, far_sum, 0)
        cols = slice(p * PW, (p + 1) * PW)
        at = pl.ds(pl.multiple_of(s * HW + p * PW, LANES), PW)
        out[0, my_rows, cols] = (rs[:, at] + sown[2 * z + p, my_rows, :]).astype(BF16)
        out[0, other_rows, cols] = (rr[:, cols] + sown[2 * z + p, other_rows, :]).astype(BF16)

    for p in range(2):
        fy_copy(p).wait_send()
    for k in range(1, n):
        rt_copy(k).wait_send()

    for h in range(LKV):
        for k in range(steps + 1):
            if k < steps:
                @pl.when(sends_z(k))
                def _():
                    kv_z(k, h).wait_send()

            @pl.when(sends_y(k))
            def _():
                kv_y(k, h).wait_send()
    for k in range(1, nd):
        dp_copy(k).wait_send()
        pg_copy(k).wait_send()
    head_copy.wait_send()
    resid_copy.wait_send()
    for zi in range(nz):
        for h in range(CH):
            @pl.when((zi <= z) & (z + 1 < nz))
            def _():
                up_copy(zi, h).wait_send()

            @pl.when((zi >= z) & (z >= 1))
            def _():
                down_copy(zi, h).wait_send()

            y_copy(zi, h).wait_send()
            p_copy(2 * zi, h).wait_send()
            p_copy(2 * zi + 1, h).wait_send()

        for p in range(2):
            @pl.when(near(zi))
            def _():
                near_copy(zi, p).wait_send()

            @pl.when((zi != z) & ~near(zi))
            def _():
                yr_copy(zi, p).wait_send()
                zr_copy(zi, p).wait_send()

        for p in range(2):
            sec_copy(zi, p).wait_send()


def trig(count):
    half = HEAD_WIDTH // 2
    frequency = np.float32(10000.0) ** (
        -(np.arange(half, dtype=np.float32) * np.float32(2.0) / np.float32(HEAD_WIDTH))
    )
    angles = np.arange(count, dtype=np.float32)[:, None] * frequency.astype(np.float32)[None, :]
    reps = LANES // half
    wide = np.tile(angles.astype(np.float64), (1, reps))
    return np.cos(wide).astype(np.float32), np.sin(wide).astype(np.float32)


def shards(
    tokens, segments, attn_gain, query_weight, key_value_weight, out_weight, ffn_gain,
    gate_weight, up_weight, down_weight, expert_ids, route_weight, stream_page_table,
):
    n = lax.axis_size("expert")
    nd = lax.axis_size("dp")
    win = n // 2
    nz = n // 2
    T, W = tokens.shape[1], tokens.shape[2]
    H, HW = T // 2, W // 2
    EL, _, FL = gate_weight.shape
    qw, kw = query_weight.shape[1], key_value_weight.shape[1]
    cosine, sine = trig(T * n)
    down = down_weight.reshape(EL * FL, W)
    vmem = pl.BlockSpec(memory_space=pltpu.VMEM)
    hbm = pl.BlockSpec(memory_space=pl.ANY)
    dma = pltpu.SemaphoreType.DMA
    out, cache = pl.pallas_call(
        functools.partial(layer_kernel, n, nd, win),
        out_shape=(
            jax.ShapeDtypeStruct((1, T, HW), BF16),
            jax.ShapeDtypeStruct((1, T, kw), BF16),
        ),
        in_specs=[vmem] * 7 + [hbm] * 8,
        out_specs=(vmem, vmem),
        scratch_shapes=[
            pltpu.VMEM((W, qw), BF16),
            pltpu.VMEM((W, kw), BF16),
            pltpu.VMEM((qw, W), BF16),
            pltpu.VMEM((EL, W, FL), BF16),
            pltpu.VMEM((EL, W, FL), BF16),
            pltpu.VMEM((EL * FL, W), BF16),
            pltpu.VMEM((T, LANES), F32),
            pltpu.VMEM((T, LANES), F32),
            pltpu.VMEM((n, 8, T), F32),
            pltpu.VMEM((n, 8, T), F32),
            pltpu.VMEM((T, W), BF16),
            pltpu.VMEM((win + 1, kw // LANES, T, LANES), BF16),
            pltpu.VMEM((nd - 1, kw // LANES, T, LANES), BF16),
            pltpu.VMEM((8, LANES), F32),
            pltpu.VMEM((nd - 1, 8, LANES), F32),
            pltpu.VMEM((T, qw), F32),
            pltpu.VMEM((T, (win + 1) * T), F32),
            pltpu.VMEM((T, qw), BF16),
            pltpu.VMEM((T, W), F32),
            pltpu.VMEM((H, W), BF16),
            pltpu.VMEM((H, W), BF16),
            pltpu.VMEM((H, W), F32),
            pltpu.VMEM((H, HW), F32),
            pltpu.VMEM((n * T, W), BF16),
            pltpu.VMEM((2 * T, EL * FL), BF16),
            pltpu.VMEM((2 * nz, 2 * T, HW // 2), BF16),
            pltpu.VMEM((2 * nz, 2 * T, HW // 2), BF16),
            pltpu.VMEM((2 * nz, 2 * T, HW // 2), F32),
            pltpu.VMEM((2 * nz, T, HW // 2), BF16),
            pltpu.VMEM((2 * nz, T, HW // 2), BF16),
            pltpu.VMEM((2 * nz, T, HW // 2), F32),
            pltpu.VMEM((2 * nz, T, HW // 2), BF16),
            pltpu.VMEM((2 * nz, T, HW // 2), BF16),
            pltpu.VMEM((4, 2 * T, HW // 2), BF16),
            pltpu.VMEM((4, 2 * T, HW // 2), BF16),
            pltpu.VMEM((2, T, HW // 2), BF16),
            pltpu.VMEM((2, T, HW // 2), BF16),
            dma((8,)),
            dma((win // 2 * (kw // LANES),)), dma(((win // 2 + 1) * (kw // LANES),)), dma((win * (kw // LANES),)),
            dma((nd - 1,)), dma((nd - 1,)), dma((nd - 1,)), dma((nd - 1,)),
            dma((2,)), dma((2,)),
            dma((nz * GATHER_CHUNKS,)), dma((nz * GATHER_CHUNKS,)), dma((nz * GATHER_CHUNKS,)),
            dma((n * GATHER_CHUNKS,)), dma((2 * n * GATHER_CHUNKS,)),
            dma((n,)), dma((n,)), dma((n,)), dma((n,)), dma((n,)), dma((n,)),
            dma((4,)), dma((4,)), dma((2,)), dma((2,)), dma((n,)), dma((n,)),
        ],
        compiler_params=pltpu.CompilerParams(
            collective_id=0, has_side_effects=True, vmem_limit_bytes=58 * 1024 * 1024
        ),
    )(
        tokens, segments, attn_gain, ffn_gain, expert_ids.transpose(0, 2, 1),
        route_weight.transpose(0, 2, 1), stream_page_table, jnp.asarray(cosine), jnp.asarray(sine),
        query_weight, key_value_weight, out_weight, gate_weight, up_weight, down,
    )

    def hand_over(out_in, cache_in, out_to, cache_to):
        out_to[...] = out_in[...]
        cache_to[...] = cache_in[...]

    return pl.pallas_call(
        hand_over,
        out_shape=(jax.ShapeDtypeStruct(out.shape, BF16), jax.ShapeDtypeStruct(cache.shape, BF16)),
        in_specs=[vmem, vmem],
        out_specs=(vmem, vmem),
    )(out, cache)


def solution(mesh):
    in_specs = (
        P("dp", "expert", None),
        P("dp", "expert"),
        P(),
        P(None, "section"),
        P(None, "section"),
        P("section", None),
        P(),
        P("expert", None, "section"),
        P("expert", None, "section"),
        P("expert", "section", None),
        P("dp", "expert", None),
        P("dp", "expert", None),
        P("dp", "expert"),
    )
    out_specs = (P("dp", "expert", "section"), P(("dp", "expert"), None, "section"))
    return jax.shard_map(shards, mesh=mesh, in_specs=in_specs, out_specs=out_specs, check_vma=False)
```
